512 devices in a mesh: pipe: 32 (over z_lo, y, core), tensor: 16 (over z_hi, x).
Axes of the slice: x: 4, y: 8, z: 8 (z_hi: 4, z_lo: 2; z = z_hi * 2 + z_lo), core: 2. Of those that a mesh axis runs over, the one named last changes fastest.
Arguments:
- tokens: bfloat16 [256, 8192], P('pipe', 'tensor'), may hold values from -6 to 6
- gate_weight: bfloat16 [8192, 28672], P('tensor', 'pipe'), may hold values from -0.0625 to 0.0625
- upward_weight: bfloat16 [8192, 28672], P('tensor', 'pipe'), may hold values from -0.0625 to 0.0625
- down_weight: bfloat16 [28672, 8192], P('pipe', 'tensor'), may hold values from -0.03125 to 0.03125
- adapter_first_factors: bfloat16 [2, 8192, 64], P(None, 'tensor'), may hold values from -0.0625 to 0.0625
- adapter_second_factors: bfloat16 [2, 64, 28672], P(None, None, 'pipe'), may hold values from -0.75 to 0.75
- adapter_of_block: int32 [2], replicated, may hold values from 0 to 1, each once
- cotangent: bfloat16 [256, 8192], P('pipe', 'tensor'), may hold values from -6 to 6
Outputs:
- mixed: bfloat16 [256, 8192], P('pipe', 'tensor')
- grad_tokens: bfloat16 [256, 8192], P('pipe', 'tensor')
- grad_a: float32 [2, 8192, 64], P(None, 'tensor')
- grad_b: float32 [2, 64, 28672], P(None, None, 'pipe')
The draws below stay inside these ranges and needn't reach their ends.
Inputs may be any that keep to these rules, and one draw needn't show every extreme that they name: `adapter_of_block`: each of the 2 adapters is named by exactly one block.
All inputs are finite; a program needn't handle non-finite values.
Results may differ from the reference program's by a relative error of at most 0.0052.
Values may be sent and summed in bfloat16 or wider, within the bound.
No kernel may reach another device: no remote copies, remote signals or barrier semaphores. Data moves between devices by JAX's collectives and lax.ppermute only.
A program may use at most 64 MiB of HBM per device.

```python
import jax
import jax.numpy as jnp
from jax import lax

MODEL_WIDTH = 8192
HIDDEN_UNITS = 28672
ADAPTER_RANK = 64
BLOCK = 128
BLOCKS = 2
ADAPTER_COUNT = 2
ROWS = 256


def steps_of(key, dims, shards, least, largest):
    gain = 1.0
    for axis_at, parts in shards:
        steps = jax.random.uniform(jax.random.fold_in(jax.random.fold_in(key, 6), axis_at), (parts,), jnp.float32, least / len(shards), largest / len(shards))
        gain = gain * jnp.repeat(jnp.exp(steps), dims[axis_at] // parts).reshape((-1,) + (1,) * (len(dims) - 1 - axis_at))
    return gain


def normal_values(rng, shape, deviation, reach, pieces=(), kind=jnp.bfloat16):
    entries = jax.random.normal(rng, shape, jnp.float32) * deviation
    if len(pieces) > 0:
        entries = steps_of(rng, shape, pieces, -0.22, 0.18) * entries
    return jnp.clip(entries, min=-reach, max=reach).astype(kind)


def setup_inputs(seed: int = 0) -> dict:
    seeds = jax.random.split(jax.random.key(seed), 9)
    tokens = normal_values(seeds[0], (ROWS, MODEL_WIDTH), 1.0, 6.0, ((0, 32), (1, 16)))
    gate_weight = normal_values(seeds[1], (MODEL_WIDTH, HIDDEN_UNITS), MODEL_WIDTH ** -0.5, 0.0625, ((0, 16), (1, 32)))
    upward_weight = normal_values(seeds[2], (MODEL_WIDTH, HIDDEN_UNITS), MODEL_WIDTH ** -0.5, 0.0625, ((0, 16), (1, 32)))
    down_weight = normal_values(seeds[3], (HIDDEN_UNITS, MODEL_WIDTH), HIDDEN_UNITS ** -0.5, 0.03125, ((0, 32), (1, 16)))
    adapter_first_factors = normal_values(seeds[4], (ADAPTER_COUNT, MODEL_WIDTH, ADAPTER_RANK), MODEL_WIDTH ** -0.5, 0.0625, ((1, 16),))
    adapter_second_factors = normal_values(seeds[5], (ADAPTER_COUNT, ADAPTER_RANK, HIDDEN_UNITS), ADAPTER_RANK ** -0.5, 0.75, ((2, 32),))
    adapter_of_block = jax.random.permutation(seeds[6], BLOCKS).astype(jnp.int32)
    cotangent = normal_values(seeds[7], (ROWS, MODEL_WIDTH), 1.0, 6.0, ((0, 32), (1, 16)))
    return dict(tokens=tokens, gate_weight=gate_weight, upward_weight=upward_weight, down_weight=down_weight, adapter_first_factors=adapter_first_factors, adapter_second_factors=adapter_second_factors, adapter_of_block=adapter_of_block, cotangent=cotangent)


adapter_scale = 0.5


def adapter_mask(row_total, adapter_of_block):
    row_index = jnp.arange(row_total, dtype=jnp.int32)
    owner = row_index // BLOCK
    block_index = jnp.arange(adapter_of_block.shape[0], dtype=jnp.int32)
    chosen = jnp.sum(jnp.where(owner[:, None] == block_index[None, :], adapter_of_block[None, :], 0), axis=1)
    columns = jnp.arange(adapter_of_block.shape[0] * ADAPTER_RANK, dtype=jnp.int32) // ADAPTER_RANK
    return (columns[None, :] == chosen[:, None]).astype(jnp.float32)


def trailing_product(left, right):
    return lax.dot_general(left, right, (((1,), (1,)), ((), ())), preferred_element_type=jnp.float32)


def reference(tokens, gate_weight, upward_weight, down_weight, adapter_first_factors, adapter_second_factors, adapter_of_block, cotangent):
    row_total = tokens.shape[0]
    adapter_total = adapter_first_factors.shape[0]
    first_factor_rows = jnp.transpose(adapter_first_factors, (1, 0, 2)).reshape(MODEL_WIDTH, adapter_total * ADAPTER_RANK)
    second_factor_rows = adapter_second_factors.reshape(adapter_total * ADAPTER_RANK, HIDDEN_UNITS)
    adapter_select_mask = adapter_mask(row_total, adapter_of_block)
    gate = jnp.dot(tokens, gate_weight, preferred_element_type=jnp.float32)
    upward_frozen_output = jnp.dot(tokens, upward_weight, preferred_element_type=jnp.float32)
    z_sum = jnp.dot(tokens, first_factor_rows, preferred_element_type=jnp.float32)
    reduced_activation = (z_sum * adapter_select_mask).astype(jnp.bfloat16)
    upward_output = upward_frozen_output + adapter_scale * jnp.dot(reduced_activation, second_factor_rows, preferred_element_type=jnp.float32)
    sig = jax.nn.sigmoid(gate)
    act = gate * sig
    hidden = (act * upward_output).astype(jnp.bfloat16)
    mixed = jnp.dot(hidden, down_weight, preferred_element_type=jnp.float32).astype(jnp.bfloat16)
    grad_hidden = trailing_product(cotangent, down_weight)
    upward_gradient = (grad_hidden * act).astype(jnp.bfloat16)
    grad_gate = (grad_hidden * upward_output * sig * (1.0 + gate * (1.0 - sig))).astype(jnp.bfloat16)
    second_factor_gradient = adapter_scale * jnp.dot(reduced_activation.T, upward_gradient, preferred_element_type=jnp.float32)
    reduced_gradient = adapter_scale * trailing_product(upward_gradient, second_factor_rows) * adapter_select_mask
    low_back = reduced_gradient.astype(jnp.bfloat16)
    back_sum = trailing_product(grad_gate, gate_weight) + trailing_product(upward_gradient, upward_weight)
    grad_tokens = (back_sum + trailing_product(low_back, first_factor_rows)).astype(jnp.bfloat16)
    grad_a_flat = jnp.dot(tokens.T, low_back, preferred_element_type=jnp.float32)
    grad_a = jnp.transpose(grad_a_flat.reshape(MODEL_WIDTH, adapter_total, ADAPTER_RANK), (1, 0, 2))
    grad_b = second_factor_gradient.reshape(adapter_total, ADAPTER_RANK, HIDDEN_UNITS)
    return mixed, grad_tokens, grad_a, grad_b
```

```python
import jax
import jax.numpy as jnp
from jax import lax
from jax.sharding import Mesh, PartitionSpec as P

PIPE = ("zlo", "y", "core")
TENSOR = ("zhi", "x")
PIPE_LINKS = ("zlo", "y")
adapter_scale = 0.5
bf16 = jnp.bfloat16
f32 = jnp.float32


def product(left, right):
    return jnp.dot(left, right, preferred_element_type=f32)


def trailing_product(left, right):
    return lax.dot_general(left, right, (((1,), (1,)), ((), ())), preferred_element_type=f32)


def leading_product(left, right):
    return lax.dot_general(left, right, (((0,), (0,)), ((), ())), preferred_element_type=f32)


def gather_rows(value, axis):
    count = lax.axis_size(axis)
    blocks = jnp.broadcast_to(value[None], (count,) + value.shape)
    return lax.all_to_all(blocks, axis, 0, 0).reshape((count * value.shape[0],) + value.shape[1:])


def scatter_sum(value, axis, sent):
    count = lax.axis_size(axis)
    blocks = value.astype(sent).reshape(count, value.shape[0] // count, value.shape[1])
    return jnp.sum(lax.all_to_all(blocks, axis, 0, 0).astype(f32), axis=0)


def on_device(
    tokens,
    gate_weight,
    upward_weight,
    down_weight,
    adapter_first_factors,
    adapter_second_factors,
    adapter_of_block,
    cotangent,
):
    adapters, width, rank = adapter_first_factors.shape
    hidden_units = gate_weight.shape[1]
    columns = adapters * rank
    first = jnp.transpose(adapter_first_factors, (1, 0, 2)).reshape(width, columns)
    second = adapter_second_factors.reshape(columns, hidden_units)

    both = jnp.concatenate([tokens, cotangent], axis=1)
    both = lax.all_gather(gather_rows(both, PIPE_LINKS), "core", axis=0, tiled=True)
    token_rows, adjoint_rows = both[:, :width], both[:, width:]

    parts = jnp.concatenate(
        [
            product(token_rows, gate_weight).astype(bf16),
            product(token_rows, upward_weight).astype(bf16),
            trailing_product(adjoint_rows, down_weight).astype(bf16),
            product(token_rows, first).astype(bf16),
        ],
        axis=1,
    )
    parts = scatter_sum(scatter_sum(parts, "x", bf16), "zhi", f32)

    def mask_of(block):
        own = jnp.arange(columns, dtype=jnp.int32) // rank
        chosen = jnp.sum(
            jnp.where(
                block[:, None] == jnp.arange(adapter_of_block.shape[0], dtype=jnp.int32)[None, :],
                adapter_of_block[None, :],
                0,
            ),
            axis=1,
        )
        return (own[None, :] == chosen[:, None]).astype(f32)

    x_index = lax.axis_index("x")
    own_mask = mask_of(jnp.full((1,), x_index % 2, jnp.int32))
    gate = parts[:, :hidden_units]
    up_base = parts[:, hidden_units : 2 * hidden_units]
    grad_hidden = parts[:, 2 * hidden_units : 3 * hidden_units]
    low = (parts[:, 3 * hidden_units :] * own_mask).astype(bf16)
    up = up_base + adapter_scale * product(low, second)
    sig = jax.nn.sigmoid(gate)
    act = gate * sig
    hidden = (act * up).astype(bf16)
    grad_up = (grad_hidden * act).astype(bf16)
    grad_gate = (grad_hidden * up * sig * (1.0 + gate * (1.0 - sig))).astype(bf16)

    rows = jnp.concatenate([hidden, grad_gate, grad_up, low], axis=1)
    rows = gather_rows(gather_rows(rows, "zhi"), "x")
    hidden_all = rows[:, :hidden_units]
    grad_gate_all = rows[:, hidden_units : 2 * hidden_units]
    grad_up_all = rows[:, 2 * hidden_units : 3 * hidden_units]
    low_all = rows[:, 3 * hidden_units :]

    row_total = rows.shape[0]
    row_block = (jnp.arange(row_total, dtype=jnp.int32) // (row_total // 4)) % 2
    all_mask = mask_of(row_block)
    partial = jnp.concatenate(
        [
            product(hidden_all, down_weight),
            trailing_product(grad_gate_all, gate_weight)
            + trailing_product(grad_up_all, upward_weight),
            adapter_scale * trailing_product(grad_up_all, second) * all_mask,
        ],
        axis=1,
    )
    summed = scatter_sum(scatter_sum(partial, "core", f32), PIPE_LINKS, bf16)
    mixed = summed[:, :width].astype(bf16)
    low_own = summed[:, 2 * width :].astype(bf16)
    grad_tokens = (summed[:, width : 2 * width] + trailing_product(low_own, first)).astype(bf16)

    grad_b = (adapter_scale * leading_product(low_all, grad_up_all)).reshape(
        adapters, rank, hidden_units
    )
    low_back = lax.all_gather(gather_rows(low_own, PIPE_LINKS), "core", axis=0, tiled=True)
    grad_a = leading_product(token_rows, low_back).reshape(width, adapters, rank)
    return mixed, grad_tokens, jnp.transpose(grad_a, (1, 0, 2)), grad_b


def solution(mesh):
    parts = Mesh(mesh.devices.reshape(2, 8, 2, 4, 4), PIPE + TENSOR)
    in_specs = (
        P(PIPE, TENSOR),
        P(TENSOR, PIPE),
        P(TENSOR, PIPE),
        P(PIPE, TENSOR),
        P(None, TENSOR, None),
        P(None, None, PIPE),
        P(),
        P(PIPE, TENSOR),
    )
    out_specs = (
        P(PIPE, TENSOR),
        P(PIPE, TENSOR),
        P(None, TENSOR, None),
        P(None, None, PIPE),
    )
    return jax.shard_map(
        on_device, mesh=parts, in_specs=in_specs, out_specs=out_specs, check_vma=False
    )
```

```python
import jax
import jax.numpy as jnp
from jax import lax
from jax.sharding import Mesh, PartitionSpec as P

PIPE = ("zlo", "y", "core")
TENSOR = ("zhi", "x")
PIPE_LINKS = ("zlo", "y")
adapter_scale = 0.5
bf16 = jnp.bfloat16
f32 = jnp.float32


def product(left, right):
    return jnp.dot(left, right, preferred_element_type=f32)


def trailing_product(left, right):
    return lax.dot_general(left, right, (((1,), (1,)), ((), ())), preferred_element_type=f32)


def leading_product(left, right):
    return lax.dot_general(left, right, (((0,), (0,)), ((), ())), preferred_element_type=f32)


def gather_rows(value, axis):
    count = lax.axis_size(axis)
    blocks = jnp.broadcast_to(value[None], (count,) + value.shape)
    return lax.all_to_all(blocks, axis, 0, 0).reshape((count * value.shape[0],) + value.shape[1:])


def scatter_sum(value, axis, sent):
    count = lax.axis_size(axis)
    blocks = value.astype(sent).reshape(count, value.shape[0] // count, value.shape[1])
    return jnp.sum(lax.all_to_all(blocks, axis, 0, 0).astype(f32), axis=0)


def on_device(
    tokens,
    gate_weight,
    upward_weight,
    down_weight,
    adapter_first_factors,
    adapter_second_factors,
    adapter_of_block,
    cotangent,
):
    adapters, width, rank = adapter_first_factors.shape
    hidden_units = gate_weight.shape[1]
    columns = adapters * rank
    first = jnp.transpose(adapter_first_factors, (1, 0, 2)).reshape(width, columns)
    second = adapter_second_factors.reshape(columns, hidden_units)

    own = jnp.arange(columns, dtype=jnp.int32) // rank
    masks = (own[None, :] == adapter_of_block[:, None]).astype(f32)
    own_mask = lax.dynamic_slice_in_dim(masks, lax.axis_index("x") % 2, 1, 0)
    block_mask = lax.dynamic_slice_in_dim(masks, lax.axis_index("zlo"), 1, 0)
    both = jnp.concatenate([tokens, cotangent], axis=1)
    own_columns = lax.axis_index("y") * columns
    masks16, block_mask = masks.astype(bf16), block_mask.astype(bf16)
    both, masks, masks16, own_mask, block_mask, own_columns = lax.optimization_barrier(
        (both, masks, masks16, own_mask, block_mask, own_columns)
    )
    both = lax.all_gather(gather_rows(both, PIPE_LINKS), "core", axis=0, tiled=True)
    token_rows, adjoint_rows = both[:, :width], both[:, width:]

    parts = jnp.concatenate(
        [
            product(token_rows, gate_weight).astype(bf16),
            product(token_rows, upward_weight).astype(bf16),
            trailing_product(adjoint_rows, down_weight).astype(bf16),
            product(token_rows, first).astype(bf16),
        ],
        axis=1,
    )
    parts = scatter_sum(scatter_sum(parts, "x", bf16), "zhi", f32)

    gate = parts[:, :hidden_units]
    up_base = parts[:, hidden_units : 2 * hidden_units]
    grad_hidden = parts[:, 2 * hidden_units : 3 * hidden_units]
    low = (parts[:, 3 * hidden_units :] * own_mask).astype(bf16)
    up = up_base + adapter_scale * product(low, second)
    sig = jax.nn.sigmoid(gate)
    act = gate * sig
    hidden = (act * up).astype(bf16)
    grad_up = (grad_hidden * act).astype(bf16)
    grad_gate = (grad_hidden * up * sig * (1.0 + gate * (1.0 - sig))).astype(bf16)

    rows = jnp.concatenate([hidden, grad_gate, grad_up, low], axis=1)
    rows = gather_rows(gather_rows(rows, "zhi"), "x")
    hidden_all = rows[:, :hidden_units]
    grad_gate_all = rows[:, hidden_units : 2 * hidden_units]
    grad_up_all = rows[:, 2 * hidden_units : 3 * hidden_units]
    low_all = rows[:, 3 * hidden_units :]

    quarter = rows.shape[0] // 4
    all_mask = jnp.broadcast_to(masks[None, :, None, :], (2, 2, quarter, columns)).reshape(
        rows.shape[0], columns
    )
    partial = jnp.concatenate(
        [
            product(hidden_all, down_weight),
            trailing_product(grad_gate_all, gate_weight)
            + trailing_product(grad_up_all, upward_weight),
            adapter_scale * trailing_product(grad_up_all, second) * all_mask,
        ],
        axis=1,
    )
    grad_b = (adapter_scale * leading_product(low_all, grad_up_all)).reshape(
        adapters, rank, hidden_units
    )
    partial, grad_b = lax.optimization_barrier((partial, grad_b))

    summed = scatter_sum(partial, "core", f32)
    packed = (summed[:quarter, 2 * width :] + summed[quarter:, 2 * width :]).astype(bf16)
    peers = lax.axis_size(PIPE_LINKS)
    wide = jnp.transpose(packed.reshape(-1, 8, columns), (1, 0, 2)).reshape(8, -1)
    sent = jnp.concatenate(
        [
            summed[:, : 2 * width].astype(bf16).reshape(peers, -1, 2 * width),
            jnp.broadcast_to(wide[None], (peers,) + wide.shape),
        ],
        axis=2,
    )
    summed = jnp.sum(lax.all_to_all(sent, PIPE_LINKS, 0, 0).astype(f32), axis=0)
    mixed = summed[:, :width].astype(bf16)
    wide = summed[:, 2 * width :].astype(bf16)
    packed = jnp.transpose(wide.reshape(8, -1, columns), (1, 0, 2)).reshape(quarter, columns)
    low_own = lax.dynamic_slice(
        wide, (0, own_columns), (8, columns), allow_negative_indices=False
    )
    low_own = low_own * block_mask
    grad_tokens = (summed[:, width : 2 * width] + trailing_product(low_own, first)).astype(bf16)

    packed = lax.all_gather(packed, "core", axis=0)
    low_back = (packed[:, None] * masks16[None, :, None, :]).reshape(-1, columns)
    grad_a = leading_product(token_rows, low_back).reshape(width, adapters, rank)
    return mixed, grad_tokens, jnp.transpose(grad_a, (1, 0, 2)), grad_b


def solution(mesh):
    parts = Mesh(mesh.devices.reshape(2, 8, 2, 4, 4), PIPE + TENSOR)
    in_specs = (
        P(PIPE, TENSOR),
        P(TENSOR, PIPE),
        P(TENSOR, PIPE),
        P(PIPE, TENSOR),
        P(None, TENSOR, None),
        P(None, None, PIPE),
        P(),
        P(PIPE, TENSOR),
    )
    out_specs = (
        P(PIPE, TENSOR),
        P(PIPE, TENSOR),
        P(None, TENSOR, None),
        P(None, None, PIPE),
    )
    return jax.shard_map(
        on_device, mesh=parts, in_specs=in_specs, out_specs=out_specs, check_vma=False
    )
```

```python
import jax
import jax.numpy as jnp
from jax import lax
from jax.sharding import Mesh, PartitionSpec as P

PIPE = ("zlo", "y", "core")
TENSOR = ("zhi", "x")
PIPE_LINKS = ("zlo", "y")
adapter_scale = 0.5
bf16 = jnp.bfloat16
f32 = jnp.float32


def product(left, right):
    return jnp.dot(left, right, preferred_element_type=f32)


def trailing_product(left, right):
    return lax.dot_general(left, right, (((1,), (1,)), ((), ())), preferred_element_type=f32)


def leading_product(left, right):
    return lax.dot_general(left, right, (((0,), (0,)), ((), ())), preferred_element_type=f32)


def gather_rows(value, axis):
    count = lax.axis_size(axis)
    blocks = jnp.broadcast_to(value[None], (count,) + value.shape)
    return lax.all_to_all(blocks, axis, 0, 0).reshape((count * value.shape[0],) + value.shape[1:])


def scatter_sum(value, axis, sent):
    count = lax.axis_size(axis)
    blocks = value.astype(sent).reshape(count, value.shape[0] // count, value.shape[1])
    return jnp.sum(lax.all_to_all(blocks, axis, 0, 0).astype(f32), axis=0)


def scatter_sum_own(pieces, axis, first_row, is_own):
    count = lax.axis_size(axis)
    rows = pieces[0].shape[0] // count
    sent = jnp.concatenate([piece.astype(bf16) for piece in pieces], axis=1)
    came = lax.all_to_all(sent.reshape(count, rows, sent.shape[1]), axis, 0, 0).astype(f32)
    own = jnp.concatenate(
        [
            lax.dynamic_slice(
                piece, (first_row, 0), (rows, piece.shape[1]), allow_negative_indices=False
            )
            for piece in pieces
        ],
        axis=1,
    )
    return jnp.sum(jnp.where(is_own[:, None, None], own[None], came), axis=0)


def on_device(
    tokens,
    gate_weight,
    upward_weight,
    down_weight,
    adapter_first_factors,
    adapter_second_factors,
    adapter_of_block,
    cotangent,
):
    adapters, width, rank = adapter_first_factors.shape
    hidden_units = gate_weight.shape[1]
    columns = adapters * rank
    first = jnp.transpose(adapter_first_factors, (1, 0, 2)).reshape(width, columns)
    second = adapter_second_factors.reshape(columns, hidden_units)

    own = jnp.arange(columns, dtype=jnp.int32) // rank
    masks = (own[None, :] == adapter_of_block[:, None]).astype(f32)
    own_mask = lax.dynamic_slice_in_dim(masks, lax.axis_index("x") % 2, 1, 0)
    block_mask = lax.dynamic_slice_in_dim(masks, lax.axis_index("zlo"), 1, 0)
    both = jnp.concatenate([tokens, cotangent], axis=1)
    own_columns = lax.axis_index("y") * columns
    masks16, block_mask = masks.astype(bf16), block_mask.astype(bf16)
    own_rows_x = lax.axis_index("x") * 64
    own_rows_z = lax.axis_index("zhi") * 16
    is_own_x = jnp.arange(4, dtype=jnp.int32) == lax.axis_index("x")
    is_own_z = jnp.arange(4, dtype=jnp.int32) == lax.axis_index("zhi")
    (
        both,
        masks,
        masks16,
        own_mask,
        block_mask,
        own_columns,
        own_rows_x,
        own_rows_z,
        is_own_x,
        is_own_z,
    ) = lax.optimization_barrier(
        (
            both,
            masks,
            masks16,
            own_mask,
            block_mask,
            own_columns,
            own_rows_x,
            own_rows_z,
            is_own_x,
            is_own_z,
        )
    )
    both = lax.all_gather(gather_rows(both, PIPE_LINKS), "core", axis=0, tiled=True)
    token_rows, adjoint_rows = both[:, :width], both[:, width:]

    pieces = [
        product(token_rows, gate_weight),
        product(token_rows, upward_weight),
        trailing_product(adjoint_rows, down_weight),
        product(token_rows, first),
    ]
    parts = scatter_sum_own(pieces, "x", own_rows_x, is_own_x)
    parts = scatter_sum_own([parts], "zhi", own_rows_z, is_own_z)

    gate = parts[:, :hidden_units]
    up_base = parts[:, hidden_units : 2 * hidden_units]
    grad_hidden = parts[:, 2 * hidden_units : 3 * hidden_units]
    low = (parts[:, 3 * hidden_units :] * own_mask).astype(bf16)
    up = up_base + adapter_scale * product(low, second)
    sig = jax.nn.sigmoid(gate)
    act = gate * sig
    hidden = (act * up).astype(bf16)
    grad_up = (grad_hidden * act).astype(bf16)
    grad_gate = (grad_hidden * up * sig * (1.0 + gate * (1.0 - sig))).astype(bf16)

    rows = jnp.concatenate([hidden, grad_gate, grad_up, low], axis=1)
    rows = gather_rows(gather_rows(rows, "zhi"), "x")
    hidden_all = rows[:, :hidden_units]
    grad_gate_all = rows[:, hidden_units : 2 * hidden_units]
    grad_up_all = rows[:, 2 * hidden_units : 3 * hidden_units]
    low_all = rows[:, 3 * hidden_units :]

    quarter = rows.shape[0] // 4
    all_mask = jnp.broadcast_to(masks[None, :, None, :], (2, 2, quarter, columns)).reshape(
        rows.shape[0], columns
    )
    partial = jnp.concatenate(
        [
            product(hidden_all, down_weight),
            trailing_product(grad_gate_all, gate_weight)
            + trailing_product(grad_up_all, upward_weight),
            adapter_scale * trailing_product(grad_up_all, second) * all_mask,
        ],
        axis=1,
    )
    grad_b = (adapter_scale * leading_product(low_all, grad_up_all)).reshape(
        adapters, rank, hidden_units
    )
    partial, grad_b = lax.optimization_barrier((partial, grad_b))

    summed = scatter_sum(partial, "core", f32)
    packed = (summed[:quarter, 2 * width :] + summed[quarter:, 2 * width :]).astype(bf16)
    peers = lax.axis_size(PIPE_LINKS)
    wide = jnp.transpose(packed.reshape(-1, 8, columns), (1, 0, 2)).reshape(8, -1)
    sent = jnp.concatenate(
        [
            summed[:, : 2 * width].astype(bf16).reshape(peers, -1, 2 * width),
            jnp.broadcast_to(wide[None], (peers,) + wide.shape),
        ],
        axis=2,
    )
    summed = jnp.sum(lax.all_to_all(sent, PIPE_LINKS, 0, 0).astype(f32), axis=0)
    mixed = summed[:, :width].astype(bf16)
    wide = summed[:, 2 * width :].astype(bf16)
    packed = jnp.transpose(wide.reshape(8, -1, columns), (1, 0, 2)).reshape(quarter, columns)
    low_own = lax.dynamic_slice(
        wide, (0, own_columns), (8, columns), allow_negative_indices=False
    )
    low_own = low_own * block_mask
    grad_tokens = (summed[:, width : 2 * width] + trailing_product(low_own, first)).astype(bf16)

    packed = lax.all_gather(packed, "core", axis=0)
    low_back = (packed[:, None] * masks16[None, :, None, :]).reshape(-1, columns)
    grad_a = leading_product(token_rows, low_back).reshape(width, adapters, rank)
    return mixed, grad_tokens, jnp.transpose(grad_a, (1, 0, 2)), grad_b


def solution(mesh):
    parts = Mesh(mesh.devices.reshape(2, 8, 2, 4, 4), PIPE + TENSOR)
    in_specs = (
        P(PIPE, TENSOR),
        P(TENSOR, PIPE),
        P(TENSOR, PIPE),
        P(PIPE, TENSOR),
        P(None, TENSOR, None),
        P(None, None, PIPE),
        P(),
        P(PIPE, TENSOR),
    )
    out_specs = (
        P(PIPE, TENSOR),
        P(PIPE, TENSOR),
        P(None, TENSOR, None),
        P(None, None, PIPE),
    )
    return jax.shard_map(
        on_device, mesh=parts, in_specs=in_specs, out_specs=out_specs, check_vma=False
    )
```

```python
import jax
import jax.numpy as jnp
from jax import lax
from jax.sharding import Mesh, PartitionSpec as P

PIPE = ("zlo", "y", "core")
TENSOR = ("zhi", "x")
PIPE_LINKS = ("zlo", "y")
adapter_scale = 0.5
bf16 = jnp.bfloat16
f32 = jnp.float32


def product(left, right):
    return jnp.dot(left, right, preferred_element_type=f32)


def trailing_product(left, right):
    return lax.dot_general(left, right, (((1,), (1,)), ((), ())), preferred_element_type=f32)


def leading_product(left, right):
    return lax.dot_general(left, right, (((0,), (0,)), ((), ())), preferred_element_type=f32)


def gather_rows(value, axis):
    count = lax.axis_size(axis)
    blocks = jnp.broadcast_to(value[None], (count,) + value.shape)
    return lax.all_to_all(blocks, axis, 0, 0).reshape((count * value.shape[0],) + value.shape[1:])


def scatter_sum(value, axis, sent):
    count = lax.axis_size(axis)
    blocks = value.astype(sent).reshape(count, value.shape[0] // count, value.shape[1])
    return jnp.sum(lax.all_to_all(blocks, axis, 0, 0).astype(f32), axis=0)


def on_device(
    tokens,
    gate_weight,
    upward_weight,
    down_weight,
    adapter_first_factors,
    adapter_second_factors,
    adapter_of_block,
    cotangent,
):
    adapters, width, rank = adapter_first_factors.shape
    hidden_units = gate_weight.shape[1]
    columns = adapters * rank
    first = jnp.transpose(adapter_first_factors, (1, 0, 2)).reshape(width, columns)
    second = adapter_second_factors.reshape(columns, hidden_units)

    own = jnp.arange(columns, dtype=jnp.int32) // rank
    masks = (own[None, :] == adapter_of_block[:, None]).astype(f32)
    own_mask = lax.dynamic_slice_in_dim(masks, lax.axis_index("x") % 2, 1, 0)
    block_mask = lax.dynamic_slice_in_dim(masks, lax.axis_index("zlo"), 1, 0)
    both = jnp.concatenate([tokens, cotangent], axis=1)
    own_columns = lax.axis_index("y") * columns
    masks16, block_mask = masks.astype(bf16), block_mask.astype(bf16)
    both, masks, masks16, own_mask, block_mask, own_columns = lax.optimization_barrier(
        (both, masks, masks16, own_mask, block_mask, own_columns)
    )
    both = lax.all_gather(gather_rows(both, PIPE_LINKS), "core", axis=0, tiled=True)
    token_rows, adjoint_rows = both[:, :width], both[:, width:]

    parts = jnp.concatenate(
        [
            product(token_rows, gate_weight).astype(bf16),
            product(token_rows, upward_weight).astype(bf16),
            trailing_product(adjoint_rows, down_weight).astype(bf16),
            product(token_rows, first).astype(bf16),
        ],
        axis=1,
    )
    groups = jnp.transpose(parts.reshape(4, 4, -1, parts.shape[1]), (1, 0, 2, 3))
    groups = groups.reshape(16, -1, parts.shape[1])
    parts = jnp.sum(lax.all_to_all(groups, TENSOR, 0, 0).astype(f32), axis=0)

    gate = parts[:, :hidden_units]
    up_base = parts[:, hidden_units : 2 * hidden_units]
    grad_hidden = parts[:, 2 * hidden_units : 3 * hidden_units]
    low = (parts[:, 3 * hidden_units :] * own_mask).astype(bf16)
    up = up_base + adapter_scale * product(low, second)
    sig = jax.nn.sigmoid(gate)
    act = gate * sig
    hidden = (act * up).astype(bf16)
    grad_up = (grad_hidden * act).astype(bf16)
    grad_gate = (grad_hidden * up * sig * (1.0 + gate * (1.0 - sig))).astype(bf16)

    rows = jnp.concatenate([hidden, grad_gate, grad_up, low], axis=1)
    rows = gather_rows(gather_rows(rows, "zhi"), "x")
    hidden_all = rows[:, :hidden_units]
    grad_gate_all = rows[:, hidden_units : 2 * hidden_units]
    grad_up_all = rows[:, 2 * hidden_units : 3 * hidden_units]
    low_all = rows[:, 3 * hidden_units :]

    quarter = rows.shape[0] // 4
    all_mask = jnp.broadcast_to(masks[None, :, None, :], (2, 2, quarter, columns)).reshape(
        rows.shape[0], columns
    )
    partial = jnp.concatenate(
        [
            product(hidden_all, down_weight),
            trailing_product(grad_gate_all, gate_weight)
            + trailing_product(grad_up_all, upward_weight),
            adapter_scale * trailing_product(grad_up_all, second) * all_mask,
        ],
        axis=1,
    )
    grad_b = (adapter_scale * leading_product(low_all, grad_up_all)).reshape(
        adapters, rank, hidden_units
    )
    partial, grad_b = lax.optimization_barrier((partial, grad_b))

    summed = scatter_sum(partial, "core", f32)
    packed = (summed[:quarter, 2 * width :] + summed[quarter:, 2 * width :]).astype(bf16)
    peers = lax.axis_size(PIPE_LINKS)
    wide = jnp.transpose(packed.reshape(-1, 8, columns), (1, 0, 2)).reshape(8, -1)
    sent = jnp.concatenate(
        [
            summed[:, : 2 * width].astype(bf16).reshape(peers, -1, 2 * width),
            jnp.broadcast_to(wide[None], (peers,) + wide.shape),
        ],
        axis=2,
    )
    summed = jnp.sum(lax.all_to_all(sent, PIPE_LINKS, 0, 0).astype(f32), axis=0)
    mixed = summed[:, :width].astype(bf16)
    wide = summed[:, 2 * width :].astype(bf16)
    packed = jnp.transpose(wide.reshape(8, -1, columns), (1, 0, 2)).reshape(quarter, columns)
    low_own = lax.dynamic_slice(
        wide, (0, own_columns), (8, columns), allow_negative_indices=False
    )
    low_own = low_own * block_mask
    grad_tokens = (summed[:, width : 2 * width] + trailing_product(low_own, first)).astype(bf16)

    packed = lax.all_gather(packed, "core", axis=0)
    low_back = (packed[:, None] * masks16[None, :, None, :]).reshape(-1, columns)
    grad_a = leading_product(token_rows, low_back).reshape(width, adapters, rank)
    return mixed, grad_tokens, jnp.transpose(grad_a, (1, 0, 2)), grad_b


def solution(mesh):
    parts = Mesh(mesh.devices.reshape(2, 8, 2, 4, 4), PIPE + TENSOR)
    in_specs = (
        P(PIPE, TENSOR),
        P(TENSOR, PIPE),
        P(TENSOR, PIPE),
        P(PIPE, TENSOR),
        P(None, TENSOR, None),
        P(None, None, PIPE),
        P(),
        P(PIPE, TENSOR),
    )
    out_specs = (
        P(PIPE, TENSOR),
        P(PIPE, TENSOR),
        P(None, TENSOR, None),
        P(None, None, PIPE),
    )
    return jax.shard_map(
        on_device, mesh=parts, in_specs=in_specs, out_specs=out_specs, check_vma=False
    )
```

```python
import jax
import jax.numpy as jnp
from jax import lax
from jax.sharding import Mesh, PartitionSpec as P

PIPE = ("zlo", "y", "core")
TENSOR = ("zhi", "x")
PIPE_LINKS = ("zlo", "y")
adapter_scale = 0.5
bf16 = jnp.bfloat16
f32 = jnp.float32


def product(left, right):
    return jnp.dot(left, right, preferred_element_type=f32)


def trailing_product(left, right):
    return lax.dot_general(left, right, (((1,), (1,)), ((), ())), preferred_element_type=f32)


def leading_product(left, right):
    return lax.dot_general(left, right, (((0,), (0,)), ((), ())), preferred_element_type=f32)


def gather_rows(value, axis):
    count = lax.axis_size(axis)
    blocks = jnp.broadcast_to(value[None], (count,) + value.shape)
    return lax.all_to_all(blocks, axis, 0, 0).reshape((count * value.shape[0],) + value.shape[1:])


def scatter_sum(value, axis, sent):
    count = lax.axis_size(axis)
    blocks = value.astype(sent).reshape(count, value.shape[0] // count, value.shape[1])
    return jnp.sum(lax.all_to_all(blocks, axis, 0, 0).astype(f32), axis=0)


def on_device(
    tokens,
    gate_weight,
    upward_weight,
    down_weight,
    adapter_first_factors,
    adapter_second_factors,
    adapter_of_block,
    cotangent,
):
    adapters, width, rank = adapter_first_factors.shape
    hidden_units = gate_weight.shape[1]
    columns = adapters * rank
    first = jnp.transpose(adapter_first_factors, (1, 0, 2)).reshape(width, columns)
    second = adapter_second_factors.reshape(columns, hidden_units)

    both = jnp.concatenate([tokens, cotangent], axis=1)
    both = lax.all_gather(gather_rows(both, PIPE_LINKS), "core", axis=0, tiled=True)
    both, adapter_of_block = lax.optimization_barrier((both, adapter_of_block))
    token_rows, adjoint_rows = both[:, :width], both[:, width:]

    def hidden_parts(row_pair):
        token_part, adjoint_part = row_pair[:, :width], row_pair[:, width:]
        return [
            product(token_part, gate_weight),
            product(token_part, upward_weight),
            trailing_product(adjoint_part, down_weight),
            product(token_part, first),
        ]

    own = jnp.arange(columns, dtype=jnp.int32) // rank
    masks = (own[None, :] == adapter_of_block[:, None]).astype(f32)
    own_mask = lax.dynamic_slice_in_dim(masks, lax.axis_index("x") % 2, 1, 0)
    masks16 = masks.astype(bf16)
    block_mask = lax.dynamic_slice_in_dim(masks16, lax.axis_index("zlo"), 1, 0)
    own_columns = lax.axis_index("y") * columns
    own_rows_z = lax.axis_index("zhi") * 16
    fours = jnp.arange(4, dtype=jnp.int32)
    peers_x = (fours != lax.axis_index("x")).astype(f32).reshape(4, 1, 1)
    peers_z = (fours != lax.axis_index("zhi")).astype(f32).reshape(4, 1, 1)

    sent = jnp.concatenate([part.astype(bf16) for part in hidden_parts(both)], axis=1)
    own_both = lax.dynamic_slice(
        both, (lax.axis_index("x") * 64, 0), (64, both.shape[1]), allow_negative_indices=False
    )
    own_parts = jnp.concatenate(hidden_parts(own_both), axis=1)
    came = lax.all_to_all(sent.reshape(4, 64, -1), "x", 0, 0)
    (
        came,
        own_parts,
        masks,
        masks16,
        own_mask,
        block_mask,
        own_columns,
        own_rows_z,
        peers_x,
        peers_z,
    ) = lax.optimization_barrier(
        (
            came,
            own_parts,
            masks,
            masks16,
            own_mask,
            block_mask,
            own_columns,
            own_rows_z,
            peers_x,
            peers_z,
        )
    )
    parts = own_parts + jnp.sum(came.astype(f32) * peers_x, axis=0)
    came = lax.all_to_all(parts.astype(bf16).reshape(4, 16, -1), "zhi", 0, 0)
    came, parts = lax.optimization_barrier((came, parts))
    own_parts = lax.dynamic_slice(
        parts, (own_rows_z, 0), (16, parts.shape[1]), allow_negative_indices=False
    )
    parts = own_parts + jnp.sum(came.astype(f32) * peers_z, axis=0)

    gate = parts[:, :hidden_units]
    up_base = parts[:, hidden_units : 2 * hidden_units]
    grad_hidden = parts[:, 2 * hidden_units : 3 * hidden_units]
    low = (parts[:, 3 * hidden_units :] * own_mask).astype(bf16)
    up = up_base + adapter_scale * product(low, second)
    sig = jax.nn.sigmoid(gate)
    act = gate * sig
    hidden = (act * up).astype(bf16)
    grad_up = (grad_hidden * act).astype(bf16)
    grad_gate = (grad_hidden * up * sig * (1.0 + gate * (1.0 - sig))).astype(bf16)

    rows = jnp.concatenate([hidden, grad_gate, grad_up, low], axis=1)
    rows = gather_rows(gather_rows(rows, "zhi"), "x")
    hidden_all = rows[:, :hidden_units]
    grad_gate_all = rows[:, hidden_units : 2 * hidden_units]
    grad_up_all = rows[:, 2 * hidden_units : 3 * hidden_units]
    low_all = rows[:, 3 * hidden_units :]

    quarter = rows.shape[0] // 4
    all_mask = jnp.broadcast_to(masks[None, :, None, :], (2, 2, quarter, columns)).reshape(
        rows.shape[0], columns
    )
    partial = jnp.concatenate(
        [
            product(hidden_all, down_weight),
            trailing_product(grad_gate_all, gate_weight)
            + trailing_product(grad_up_all, upward_weight),
            adapter_scale * trailing_product(grad_up_all, second) * all_mask,
        ],
        axis=1,
    )
    grad_b = (adapter_scale * leading_product(low_all, grad_up_all)).reshape(
        adapters, rank, hidden_units
    )
    partial, grad_b = lax.optimization_barrier((partial, grad_b))

    summed = scatter_sum(partial, "core", f32)
    packed = (summed[:quarter, 2 * width :] + summed[quarter:, 2 * width :]).astype(bf16)
    peers = lax.axis_size(PIPE_LINKS)
    wide = jnp.transpose(packed.reshape(-1, 8, columns), (1, 0, 2)).reshape(8, -1)
    sent = jnp.concatenate(
        [
            summed[:, : 2 * width].astype(bf16).reshape(peers, -1, 2 * width),
            jnp.broadcast_to(wide[None], (peers,) + wide.shape),
        ],
        axis=2,
    )
    summed = jnp.sum(lax.all_to_all(sent, PIPE_LINKS, 0, 0).astype(f32), axis=0)
    mixed = summed[:, :width].astype(bf16)
    wide = summed[:, 2 * width :].astype(bf16)
    packed = jnp.transpose(wide.reshape(8, -1, columns), (1, 0, 2)).reshape(quarter, columns)
    low_own = lax.dynamic_slice(
        wide, (0, own_columns), (8, columns), allow_negative_indices=False
    )
    low_own = low_own * block_mask
    grad_tokens = (summed[:, width : 2 * width] + trailing_product(low_own, first)).astype(bf16)

    packed = lax.all_gather(packed, "core", axis=0)
    low_back = (packed[:, None] * masks16[None, :, None, :]).reshape(-1, columns)
    grad_a = leading_product(token_rows, low_back).reshape(width, adapters, rank)
    return mixed, grad_tokens, jnp.transpose(grad_a, (1, 0, 2)), grad_b


def solution(mesh):
    parts = Mesh(mesh.devices.reshape(2, 8, 2, 4, 4), PIPE + TENSOR)
    in_specs = (
        P(PIPE, TENSOR),
        P(TENSOR, PIPE),
        P(TENSOR, PIPE),
        P(PIPE, TENSOR),
        P(None, TENSOR, None),
        P(None, None, PIPE),
        P(),
        P(PIPE, TENSOR),
    )
    out_specs = (
        P(PIPE, TENSOR),
        P(PIPE, TENSOR),
        P(None, TENSOR, None),
        P(None, None, PIPE),
    )
    return jax.shard_map(
        on_device, mesh=parts, in_specs=in_specs, out_specs=out_specs, check_vma=False
    )
```

```python
import jax
import jax.numpy as jnp
import numpy as np
from jax import lax
from jax.sharding import Mesh, PartitionSpec as P

PIPE = ("zlo", "y", "core")
TENSOR = ("zhi", "x")
PIPE_LINKS = ("zlo", "y")
adapter_scale = 0.5
bf16 = jnp.bfloat16
f32 = jnp.float32


def product(left, right):
    return jnp.dot(left, right, preferred_element_type=f32)


def trailing_product(left, right):
    return lax.dot_general(left, right, (((1,), (1,)), ((), ())), preferred_element_type=f32)


def leading_product(left, right):
    return lax.dot_general(left, right, (((0,), (0,)), ((), ())), preferred_element_type=f32)


def gather_rows(value, axis):
    count = lax.axis_size(axis)
    blocks = jnp.broadcast_to(value[None], (count,) + value.shape)
    return lax.all_to_all(blocks, axis, 0, 0).reshape((count * value.shape[0],) + value.shape[1:])


def own_block(value, first_row, rows):
    return lax.dynamic_slice(
        value, (first_row, 0), (rows, value.shape[1]), allow_negative_indices=False
    )


def fence(*values):
    return lax.optimization_barrier(values)


def on_device(
    tokens,
    gate_weight,
    upward_weight,
    down_weight,
    adapter_first_factors,
    adapter_second_factors,
    adapter_of_block,
    cotangent,
):
    adapters, width, rank = adapter_first_factors.shape
    hidden_units = gate_weight.shape[1]
    columns = adapters * rank
    first = jnp.transpose(adapter_first_factors, (1, 0, 2)).reshape(width, columns)
    second = adapter_second_factors.reshape(columns, hidden_units)

    tokens, cotangent, *place = fence(
        tokens, cotangent, *(lax.axis_index(name) for name in ("core", "zhi", "x"))
    )
    both = jnp.concatenate([tokens, cotangent], axis=1)
    both = lax.all_gather(gather_rows(both, PIPE_LINKS), "core", axis=0, tiled=True)
    both, adapter_of_block, core, zhi, x = fence(both, adapter_of_block, *place)
    token_rows, adjoint_rows = both[:, :width], both[:, width:]

    own = np.arange(columns, dtype=np.int32) // rank
    masks = (own[None, :] == adapter_of_block[:, None]).astype(f32)
    own_mask = lax.dynamic_slice(masks, (x % 2, 0), (1, columns), allow_negative_indices=False)
    all_masks = jnp.broadcast_to(masks[None, :, None, :], (2, 2, 64, columns)).reshape(
        256, columns
    )
    fours = np.arange(4, dtype=np.int32)
    peers_x = (fours != x).astype(f32).reshape(4, 1, 1)
    peers_z = (fours != zhi).astype(f32).reshape(4, 1, 1)
    own_z, own_core, other_core = zhi * 16, core * 128, (1 - core) * 128
    core_is = jnp.stack([core == 0, core == 1]).astype(bf16).reshape(2, 1, 1)

    def hidden_parts(row_pair):
        token_part, adjoint_part = row_pair[:, :width], row_pair[:, width:]
        return [
            product(token_part, gate_weight),
            product(token_part, upward_weight),
            trailing_product(adjoint_part, down_weight),
            product(token_part, first),
        ]

    sent = jnp.concatenate([part.astype(bf16) for part in hidden_parts(both)], axis=1)
    parts = jnp.concatenate(hidden_parts(own_block(both, x * 64, 64)), axis=1)
    sent, parts, all_masks, own_mask, peers_x, peers_z, own_z, own_core, other_core, core_is = fence(
        sent, parts, all_masks, own_mask, peers_x, peers_z, own_z, own_core, other_core, core_is
    )
    came = lax.all_to_all(sent.reshape(4, 64, -1), "x", 0, 0)
    parts = parts + jnp.sum(came.astype(f32) * peers_x, axis=0)
    came = lax.all_to_all(parts.astype(bf16).reshape(4, 16, -1), "zhi", 0, 0)
    came, parts = fence(came, parts)
    parts = own_block(parts, own_z, 16) + jnp.sum(came.astype(f32) * peers_z, axis=0)

    gate = parts[:, :hidden_units]
    up_base = parts[:, hidden_units : 2 * hidden_units]
    grad_hidden = parts[:, 2 * hidden_units : 3 * hidden_units]
    low = (parts[:, 3 * hidden_units :] * own_mask).astype(bf16)
    up = up_base + adapter_scale * product(low, second)
    sig = jax.nn.sigmoid(gate)
    act = gate * sig
    hidden = (act * up).astype(bf16)
    grad_up = (grad_hidden * act).astype(bf16)
    grad_gate = (grad_hidden * up * sig * (1.0 + gate * (1.0 - sig))).astype(bf16)

    rows = jnp.concatenate([hidden, grad_gate, grad_up, low], axis=1)
    rows = gather_rows(gather_rows(rows, "zhi"), "x")
    grad_up_all = rows[:, 2 * hidden_units : 3 * hidden_units]
    low_parts = adapter_scale * trailing_product(grad_up_all, second) * all_masks
    low_parts = jnp.sum(lax.all_gather(low_parts, "core", axis=0), axis=0).astype(bf16)
    low_parts = jnp.transpose(low_parts.reshape(2, 16, 8, columns), (1, 0, 2, 3))
    low_parts, rows = fence(low_parts.reshape(16, 16, columns), rows)
    low_parts = lax.all_to_all(low_parts, PIPE_LINKS, 0, 0)

    hidden_all = rows[:, :hidden_units]
    grad_gate_all = rows[:, hidden_units : 2 * hidden_units]
    grad_up_all = rows[:, 2 * hidden_units : 3 * hidden_units]
    low_all = rows[:, 3 * hidden_units :]
    partial = jnp.concatenate(
        [
            product(hidden_all, down_weight),
            trailing_product(grad_gate_all, gate_weight)
            + trailing_product(grad_up_all, upward_weight),
        ],
        axis=1,
    )
    grad_b = (adapter_scale * leading_product(low_all, grad_up_all)).reshape(
        adapters, rank, hidden_units
    )
    swap = [(0, 1), (1, 0)]
    partial = own_block(partial, own_core, 128) + lax.ppermute(
        own_block(partial, other_core, 128), "core", swap
    )
    low_parts, partial, grad_b = fence(low_parts, partial.astype(bf16), grad_b)

    low_mine = jnp.sum(low_parts.astype(f32), axis=0).astype(bf16)
    low_own = jnp.sum(low_mine.reshape(2, 8, columns) * core_is, axis=0)
    wide = jnp.concatenate([low_mine[:8], low_mine[8:]], axis=1)
    sent = jnp.concatenate(
        [partial.reshape(16, 8, -1), jnp.broadcast_to(wide[None], (16,) + wide.shape)], axis=2
    )
    sent, low_own = fence(sent, low_own)
    came = lax.all_to_all(sent, PIPE_LINKS, 0, 0)
    came, low_own = fence(came, low_own)
    summed = jnp.sum(came[:, :, : 2 * width].astype(f32), axis=0)
    mixed = summed[:, :width].astype(bf16)
    grad_tokens = (summed[:, width:] + trailing_product(low_own, first)).astype(bf16)
    low_back = jnp.concatenate(
        [
            came[:, :, 2 * width : 2 * width + columns].reshape(128, columns),
            came[:, :, 2 * width + columns :].reshape(128, columns),
        ],
        axis=0,
    )
    grad_a = leading_product(token_rows, low_back).reshape(width, adapters, rank)
    return mixed, grad_tokens, jnp.transpose(grad_a, (1, 0, 2)), grad_b


def solution(mesh):
    parts = Mesh(mesh.devices.reshape(2, 8, 2, 4, 4), PIPE + TENSOR)
    in_specs = (
        P(PIPE, TENSOR),
        P(TENSOR, PIPE),
        P(TENSOR, PIPE),
        P(PIPE, TENSOR),
        P(None, TENSOR, None),
        P(None, None, PIPE),
        P(),
        P(PIPE, TENSOR),
    )
    out_specs = (
        P(PIPE, TENSOR),
        P(PIPE, TENSOR),
        P(None, TENSOR, None),
        P(None, None, PIPE),
    )
    return jax.shard_map(
        on_device, mesh=parts, in_specs=in_specs, out_specs=out_specs, check_vma=False
    )
```

```python
import jax
import jax.numpy as jnp
from jax import lax
from jax.sharding import Mesh, PartitionSpec as P

PIPE = ("zlo", "y", "core")
TENSOR = ("zhi", "x")
PIPE_LINKS = ("zlo", "y")
adapter_scale = 0.5
bf16 = jnp.bfloat16
f32 = jnp.float32


def product(left, right):
    return jnp.dot(left, right, preferred_element_type=f32)


def trailing_product(left, right):
    return lax.dot_general(left, right, (((1,), (1,)), ((), ())), preferred_element_type=f32)


def leading_product(left, right):
    return lax.dot_general(left, right, (((0,), (0,)), ((), ())), preferred_element_type=f32)


def gather_rows(value, axis):
    count = lax.axis_size(axis)
    blocks = jnp.broadcast_to(value[None], (count,) + value.shape)
    return lax.all_to_all(blocks, axis, 0, 0).reshape((count * value.shape[0],) + value.shape[1:])


def own_block(value, first_row, rows):
    return lax.dynamic_slice(
        value, (first_row, 0), (rows, value.shape[1]), allow_negative_indices=False
    )


def on_device(
    tokens,
    gate_weight,
    upward_weight,
    down_weight,
    adapter_first_factors,
    adapter_second_factors,
    adapter_of_block,
    cotangent,
):
    adapters, width, rank = adapter_first_factors.shape
    hidden_units = gate_weight.shape[1]
    columns = adapters * rank
    first = jnp.transpose(adapter_first_factors, (1, 0, 2)).reshape(width, columns)
    second = adapter_second_factors.reshape(columns, hidden_units)

    both = jnp.concatenate([tokens, cotangent], axis=1)
    both = lax.all_gather(gather_rows(both, PIPE_LINKS), "core", axis=0, tiled=True)
    both, adapter_of_block = lax.optimization_barrier((both, adapter_of_block))
    token_rows, adjoint_rows = both[:, :width], both[:, width:]

    def hidden_parts(row_pair):
        token_part, adjoint_part = row_pair[:, :width], row_pair[:, width:]
        return [
            product(token_part, gate_weight),
            product(token_part, upward_weight),
            trailing_product(adjoint_part, down_weight),
            product(token_part, first),
        ]

    own = jnp.arange(columns, dtype=jnp.int32) // rank
    masks = (own[None, :] == adapter_of_block[:, None]).astype(f32)
    own_mask = lax.dynamic_slice_in_dim(masks, lax.axis_index("x") % 2, 1, 0)
    masks16 = masks.astype(bf16)
    block_mask = lax.dynamic_slice_in_dim(masks16, lax.axis_index("zlo"), 1, 0)
    own_columns = lax.axis_index("y") * columns
    own_rows_z = lax.axis_index("zhi") * 16
    own_half = lax.axis_index("core") * 128
    other_half = 128 - own_half
    fours = jnp.arange(4, dtype=jnp.int32)
    peers_x = (fours != lax.axis_index("x")).astype(f32).reshape(4, 1, 1)
    peers_z = (fours != lax.axis_index("zhi")).astype(f32).reshape(4, 1, 1)

    sent = jnp.concatenate([part.astype(bf16) for part in hidden_parts(both)], axis=1)
    own_both = lax.dynamic_slice(
        both, (lax.axis_index("x") * 64, 0), (64, both.shape[1]), allow_negative_indices=False
    )
    own_parts = jnp.concatenate(hidden_parts(own_both), axis=1)
    came = lax.all_to_all(sent.reshape(4, 64, -1), "x", 0, 0)
    (
        came,
        own_parts,
        masks,
        masks16,
        own_mask,
        block_mask,
        own_columns,
        own_rows_z,
        own_half,
        other_half,
        peers_x,
        peers_z,
    ) = lax.optimization_barrier(
        (
            came,
            own_parts,
            masks,
            masks16,
            own_mask,
            block_mask,
            own_columns,
            own_rows_z,
        own_half,
        other_half,
            peers_x,
            peers_z,
        )
    )
    parts = own_parts + jnp.sum(came.astype(f32) * peers_x, axis=0)
    came = lax.all_to_all(parts.astype(bf16).reshape(4, 16, -1), "zhi", 0, 0)
    came, parts = lax.optimization_barrier((came, parts))
    own_parts = lax.dynamic_slice(
        parts, (own_rows_z, 0), (16, parts.shape[1]), allow_negative_indices=False
    )
    parts = own_parts + jnp.sum(came.astype(f32) * peers_z, axis=0)

    gate = parts[:, :hidden_units]
    up_base = parts[:, hidden_units : 2 * hidden_units]
    grad_hidden = parts[:, 2 * hidden_units : 3 * hidden_units]
    low = (parts[:, 3 * hidden_units :] * own_mask).astype(bf16)
    up = up_base + adapter_scale * product(low, second)
    sig = jax.nn.sigmoid(gate)
    act = gate * sig
    hidden = (act * up).astype(bf16)
    grad_up = (grad_hidden * act).astype(bf16)
    grad_gate = (grad_hidden * up * sig * (1.0 + gate * (1.0 - sig))).astype(bf16)

    rows = jnp.concatenate([hidden, grad_gate, grad_up, low], axis=1)
    rows = gather_rows(gather_rows(rows, "zhi"), "x")
    hidden_all = rows[:, :hidden_units]
    grad_gate_all = rows[:, hidden_units : 2 * hidden_units]
    grad_up_all = rows[:, 2 * hidden_units : 3 * hidden_units]
    low_all = rows[:, 3 * hidden_units :]

    quarter = rows.shape[0] // 4
    all_mask = jnp.broadcast_to(masks[None, :, None, :], (2, 2, quarter, columns)).reshape(
        rows.shape[0], columns
    )
    partial = jnp.concatenate(
        [
            product(hidden_all, down_weight),
            trailing_product(grad_gate_all, gate_weight)
            + trailing_product(grad_up_all, upward_weight),
            adapter_scale * trailing_product(grad_up_all, second) * all_mask,
        ],
        axis=1,
    )
    grad_b = (adapter_scale * leading_product(low_all, grad_up_all)).reshape(
        adapters, rank, hidden_units
    )
    summed = own_block(partial, own_half, 128) + lax.ppermute(
        own_block(partial, other_half, 128), "core", [(0, 1), (1, 0)]
    )
    summed, grad_b = lax.optimization_barrier((summed, grad_b))

    packed = (summed[:quarter, 2 * width :] + summed[quarter:, 2 * width :]).astype(bf16)
    peers = lax.axis_size(PIPE_LINKS)
    wide = jnp.transpose(packed.reshape(-1, 8, columns), (1, 0, 2)).reshape(8, -1)
    sent = jnp.concatenate(
        [
            summed[:, : 2 * width].astype(bf16).reshape(peers, -1, 2 * width),
            jnp.broadcast_to(wide[None], (peers,) + wide.shape),
        ],
        axis=2,
    )
    summed = jnp.sum(lax.all_to_all(sent, PIPE_LINKS, 0, 0).astype(f32), axis=0)
    mixed = summed[:, :width].astype(bf16)
    wide = summed[:, 2 * width :].astype(bf16)
    packed = jnp.transpose(wide.reshape(8, -1, columns), (1, 0, 2)).reshape(quarter, columns)
    low_own = lax.dynamic_slice(
        wide, (0, own_columns), (8, columns), allow_negative_indices=False
    )
    low_own = low_own * block_mask
    grad_tokens = (summed[:, width : 2 * width] + trailing_product(low_own, first)).astype(bf16)

    packed = lax.all_gather(packed, "core", axis=0)
    low_back = (packed[:, None] * masks16[None, :, None, :]).reshape(-1, columns)
    grad_a = leading_product(token_rows, low_back).reshape(width, adapters, rank)
    return mixed, grad_tokens, jnp.transpose(grad_a, (1, 0, 2)), grad_b


def solution(mesh):
    parts = Mesh(mesh.devices.reshape(2, 8, 2, 4, 4), PIPE + TENSOR)
    in_specs = (
        P(PIPE, TENSOR),
        P(TENSOR, PIPE),
        P(TENSOR, PIPE),
        P(PIPE, TENSOR),
        P(None, TENSOR, None),
        P(None, None, PIPE),
        P(),
        P(PIPE, TENSOR),
    )
    out_specs = (
        P(PIPE, TENSOR),
        P(PIPE, TENSOR),
        P(None, TENSOR, None),
        P(None, None, PIPE),
    )
    return jax.shard_map(
        on_device, mesh=parts, in_specs=in_specs, out_specs=out_specs, check_vma=False
    )
```

```python
import jax
import jax.numpy as jnp
from jax import lax
from jax.experimental import pallas as pl
from jax.experimental.pallas import tpu as pltpu
from jax.sharding import Mesh, PartitionSpec as P

PIPE = ("zlo", "y", "core")
TENSOR = ("zhi", "x")
PIPE_LINKS = ("zlo", "y")
adapter_scale = 0.5
bf16 = jnp.bfloat16
f32 = jnp.float32


def product(left, right):
    return jnp.dot(left, right, preferred_element_type=f32)


def trailing_product(left, right):
    return lax.dot_general(left, right, (((1,), (1,)), ((), ())), preferred_element_type=f32)


def leading_product(left, right):
    return lax.dot_general(left, right, (((0,), (0,)), ((), ())), preferred_element_type=f32)


def gather_rows(value, axis):
    count = lax.axis_size(axis)
    blocks = jnp.broadcast_to(value[None], (count,) + value.shape)
    return lax.all_to_all(blocks, axis, 0, 0).reshape((count * value.shape[0],) + value.shape[1:])


def own_block(value, first_row, rows):
    return lax.dynamic_slice(
        value, (first_row, 0), (rows, value.shape[1]), allow_negative_indices=False
    )


def on_chip(kernel, out_shape, scalars, *arrays, scratch=()):
    return pl.pallas_call(
        kernel,
        out_shape=out_shape,
        in_specs=[pl.BlockSpec(memory_space=pltpu.SMEM)] * len(scalars)
        + [pl.BlockSpec(memory_space=pltpu.VMEM)] * len(arrays),
        out_specs=[pl.BlockSpec(memory_space=pltpu.VMEM)] * len(out_shape),
        scratch_shapes=scratch,
        compiler_params=pltpu.CompilerParams(vmem_limit_bytes=40 * 2**20),
    )(*scalars, *arrays)


def first_products(both, gate, up, down, first, sent, own, product_of):
    width, units = gate.shape
    own_rows = own.shape[0]
    start = pl.multiple_of(lax.axis_index("x") * own_rows, own_rows)

    def put(value, at):
        size = value.shape[1]
        product_of[:, :size] = value
        sent[:, at : at + size] = value.astype(bf16)
        own[:, at : at + size] = product_of[pl.ds(start, own_rows), :size]

    for at in range(0, units, 256):
        to = min(at + 256, units)
        put(product(both[:, :width], gate[:, at:to]), at)
        put(product(both[:, :width], up[:, at:to]), units + at)
        put(trailing_product(both[:, width:], down[at:to, :]), 2 * units + at)
    put(trailing_product(both[:, :width], first[...]), 3 * units)


def sum_of_blocks(came, own, index, rows):
    total = own
    for peer in range(came.shape[0]):
        factor = jnp.where(index == peer, 0.0, 1.0).astype(f32)
        total = total + came[peer, rows, :].astype(f32) * factor
    return total


def middle_sum(came, own, sent, next_own):
    x, zhi = lax.axis_index("x"), lax.axis_index("zhi")
    size = next_own.shape[0]
    for block in range(own.shape[0] // size):
        rows = pl.ds(block * size, size)
        total = sum_of_blocks(came, own[rows, :], x, rows)
        sent[rows, :] = total.astype(bf16)

        @pl.when(zhi == block)
        def _():
            next_own[...] = total


def elementwise(adapter_of_block, came, own, second, rows):
    columns, units = second.shape
    size = own.shape[0]
    whole = sum_of_blocks(came, own[...], lax.axis_index("zhi"), pl.ds(0, size))
    adapter = adapter_of_block[lax.rem(lax.axis_index("x"), 2)]
    column = lax.broadcasted_iota(jnp.int32, (size, columns), 1)
    chosen = (column >= adapter * (columns // 2)) & (column < (adapter + 1) * (columns // 2))
    low = jnp.where(chosen, whole[:, 3 * units :], 0.0).astype(bf16)
    gate = whole[:, :units]
    grad_hidden = whole[:, 2 * units : 3 * units]
    up = whole[:, units : 2 * units] + adapter_scale * product(low, second[...])
    sig = jax.nn.sigmoid(gate)
    act = gate * sig
    hidden = (act * up).astype(bf16)
    grad_up = (grad_hidden * act).astype(bf16)
    grad_gate = (grad_hidden * up * sig * (1.0 + gate * (1.0 - sig))).astype(bf16)
    for copy in range(rows.shape[0]):
        rows[copy, :, :units] = hidden
        rows[copy, :, units : 2 * units] = grad_gate
        rows[copy, :, 2 * units : 3 * units] = grad_up
        rows[copy, :, 3 * units :] = low


def on_device(
    tokens,
    gate_weight,
    upward_weight,
    down_weight,
    adapter_first_factors,
    adapter_second_factors,
    adapter_of_block,
    cotangent,
):
    adapters, width, rank = adapter_first_factors.shape
    hidden_units = gate_weight.shape[1]
    columns = adapters * rank
    first = jnp.transpose(adapter_first_factors, (1, 0, 2)).reshape(width, columns)
    second = adapter_second_factors.reshape(columns, hidden_units)

    both = jnp.concatenate([tokens, cotangent], axis=1)
    both = lax.all_gather(gather_rows(both, PIPE_LINKS), "core", axis=0, tiled=True)
    token_rows = both[:, :width]
    row_total = both.shape[0]
    all_columns = 3 * hidden_units + columns

    first_flat = jnp.transpose(adapter_first_factors, (0, 2, 1)).reshape(columns, width)
    sent, own = on_chip(
        first_products,
        [
            jax.ShapeDtypeStruct((row_total, all_columns), bf16),
            jax.ShapeDtypeStruct((row_total // 4, all_columns), f32),
        ],
        [],
        both,
        gate_weight,
        upward_weight,
        down_weight,
        first_flat,
        scratch=[pltpu.VMEM((row_total, 256), f32)],
    )
    came = lax.all_to_all(sent.reshape(4, row_total // 4, -1), "x", 0, 0)
    sent, own = on_chip(
        middle_sum,
        [
            jax.ShapeDtypeStruct((row_total // 4, all_columns), bf16),
            jax.ShapeDtypeStruct((row_total // 16, all_columns), f32),
        ],
        [],
        came,
        own,
    )
    came = lax.all_to_all(sent.reshape(4, row_total // 16, -1), "zhi", 0, 0)
    (rows,) = on_chip(
        elementwise,
        [jax.ShapeDtypeStruct((4, row_total // 16, all_columns), bf16)],
        [adapter_of_block],
        came,
        own,
        second,
    )
    rows = lax.all_to_all(rows, "zhi", 0, 0).reshape(row_total // 4, -1)
    rows = gather_rows(rows, "x")

    own = jnp.arange(columns, dtype=jnp.int32) // rank
    masks = (own[None, :] == adapter_of_block[:, None]).astype(f32)
    masks16 = masks.astype(bf16)
    block_mask = lax.dynamic_slice_in_dim(masks16, lax.axis_index("zlo"), 1, 0)
    own_columns = lax.axis_index("y") * columns
    own_half = lax.axis_index("core") * 128
    other_half = 128 - own_half
    (
        rows,
        masks,
        masks16,
        block_mask,
        own_columns,
        own_half,
        other_half,
    ) = lax.optimization_barrier(
        (rows, masks, masks16, block_mask, own_columns, own_half, other_half)
    )
    hidden_all = rows[:, :hidden_units]
    grad_gate_all = rows[:, hidden_units : 2 * hidden_units]
    grad_up_all = rows[:, 2 * hidden_units : 3 * hidden_units]
    low_all = rows[:, 3 * hidden_units :]

    quarter = rows.shape[0] // 4
    all_mask = jnp.broadcast_to(masks[None, :, None, :], (2, 2, quarter, columns)).reshape(
        rows.shape[0], columns
    )
    partial = jnp.concatenate(
        [
            product(hidden_all, down_weight),
            trailing_product(grad_gate_all, gate_weight)
            + trailing_product(grad_up_all, upward_weight),
            adapter_scale * trailing_product(grad_up_all, second) * all_mask,
        ],
        axis=1,
    )
    grad_b = (adapter_scale * leading_product(low_all, grad_up_all)).reshape(
        adapters, rank, hidden_units
    )
    summed = own_block(partial, own_half, 128) + lax.ppermute(
        own_block(partial, other_half, 128), "core", [(0, 1), (1, 0)]
    )
    summed, grad_b = lax.optimization_barrier((summed, grad_b))

    packed = (summed[:quarter, 2 * width :] + summed[quarter:, 2 * width :]).astype(bf16)
    peers = lax.axis_size(PIPE_LINKS)
    wide = jnp.transpose(packed.reshape(-1, 8, columns), (1, 0, 2)).reshape(8, -1)
    sent = jnp.concatenate(
        [
            summed[:, : 2 * width].astype(bf16).reshape(peers, -1, 2 * width),
            jnp.broadcast_to(wide[None], (peers,) + wide.shape),
        ],
        axis=2,
    )
    summed = jnp.sum(lax.all_to_all(sent, PIPE_LINKS, 0, 0).astype(f32), axis=0)
    mixed = summed[:, :width].astype(bf16)
    wide = summed[:, 2 * width :].astype(bf16)
    packed = jnp.transpose(wide.reshape(8, -1, columns), (1, 0, 2)).reshape(quarter, columns)
    low_own = lax.dynamic_slice(
        wide, (0, own_columns), (8, columns), allow_negative_indices=False
    )
    low_own = low_own * block_mask
    grad_tokens = (summed[:, width : 2 * width] + trailing_product(low_own, first)).astype(bf16)

    packed = lax.all_gather(packed, "core", axis=0)
    low_back = (packed[:, None] * masks16[None, :, None, :]).reshape(-1, columns)
    grad_a = leading_product(token_rows, low_back).reshape(width, adapters, rank)
    return mixed, grad_tokens, jnp.transpose(grad_a, (1, 0, 2)), grad_b


def solution(mesh):
    parts = Mesh(mesh.devices.reshape(2, 8, 2, 4, 4), PIPE + TENSOR)
    in_specs = (
        P(PIPE, TENSOR),
        P(TENSOR, PIPE),
        P(TENSOR, PIPE),
        P(PIPE, TENSOR),
        P(None, TENSOR, None),
        P(None, None, PIPE),
        P(),
        P(PIPE, TENSOR),
    )
    out_specs = (
        P(PIPE, TENSOR),
        P(PIPE, TENSOR),
        P(None, TENSOR, None),
        P(None, None, PIPE),
    )
    return jax.shard_map(
        on_device, mesh=parts, in_specs=in_specs, out_specs=out_specs, check_vma=False
    )
```

```python
import jax
import jax.numpy as jnp
from jax import lax
from jax.experimental import pallas as pl
from jax.experimental.pallas import tpu as pltpu
from jax.sharding import Mesh, PartitionSpec as P

PIPE = ("zlo", "y", "core")
TENSOR = ("zhi", "x")
PIPE_LINKS = ("zlo", "y")
adapter_scale = 0.5
bf16 = jnp.bfloat16
f32 = jnp.float32


def product(left, right):
    return jnp.dot(left, right, preferred_element_type=f32)


def trailing_product(left, right):
    return lax.dot_general(left, right, (((1,), (1,)), ((), ())), preferred_element_type=f32)


def leading_product(left, right):
    return lax.dot_general(left, right, (((0,), (0,)), ((), ())), preferred_element_type=f32)


def gather_rows(value, axis):
    count = lax.axis_size(axis)
    blocks = jnp.broadcast_to(value[None], (count,) + value.shape)
    return lax.all_to_all(blocks, axis, 0, 0).reshape((count * value.shape[0],) + value.shape[1:])


def own_block(value, first_row, rows):
    return lax.dynamic_slice(
        value, (first_row, 0), (rows, value.shape[1]), allow_negative_indices=False
    )


def on_chip(kernel, out_shape, scalars, arrays, far=(), scratch=()):
    return pl.pallas_call(
        kernel,
        out_shape=out_shape,
        in_specs=[pl.BlockSpec(memory_space=pltpu.SMEM)] * len(scalars)
        + [pl.BlockSpec(memory_space=pltpu.VMEM)] * len(arrays)
        + [pl.BlockSpec(memory_space=pltpu.HBM)] * len(far),
        out_specs=[pl.BlockSpec(memory_space=pltpu.VMEM)] * len(out_shape),
        scratch_shapes=scratch,
        compiler_params=pltpu.CompilerParams(vmem_limit_bytes=40 * 2**20),
    )(*scalars, *arrays, *(pltpu.with_memory_space_constraint(array, pltpu.HBM) for array in far))


def near_and_done(*arrays):
    return [pltpu.VMEM(array.shape, array.dtype) for array in arrays] + [
        pltpu.SemaphoreType.DMA((len(arrays),))
    ]


def chosen_columns(adapter, rows, columns, rank):
    column = lax.broadcasted_iota(jnp.int32, (rows, columns), 1)
    return (column >= adapter * rank) & (column < (adapter + 1) * rank)


def first_products(both, gate, first, up_far, down_far, sent, own, product_of, up, down, done):
    fetch_up = pltpu.make_async_copy(up_far, up, done.at[0])
    fetch_down = pltpu.make_async_copy(down_far, down, done.at[1])
    fetch_up.start()
    fetch_down.start()
    width, units = gate.shape
    own_rows = own.shape[0]
    start = pl.multiple_of(lax.axis_index("x") * own_rows, own_rows)

    def put(value, at):
        size = value.shape[1]
        product_of[:, :size] = value
        sent[:, at : at + size] = value.astype(bf16)
        own[:, at : at + size] = product_of[pl.ds(start, own_rows), :size]

    chunks = [(at, min(at + 256, units)) for at in range(0, units, 256)]
    for at, to in chunks:
        put(product(both[:, :width], gate[:, at:to]), at)
    put(trailing_product(both[:, :width], first[...]), 3 * units)
    fetch_up.wait()
    for at, to in chunks:
        put(product(both[:, :width], up[:, at:to]), units + at)
    fetch_down.wait()
    for at, to in chunks:
        put(trailing_product(both[:, width:], down[at:to, :]), 2 * units + at)


def sum_of_blocks(came, own, index, rows):
    total = own
    for peer in range(came.shape[0]):
        factor = jnp.where(index == peer, 0.0, 1.0).astype(f32)
        total = total + came[peer, rows, :].astype(f32) * factor
    return total


def middle_sum(came, own, sent, next_own):
    x, zhi = lax.axis_index("x"), lax.axis_index("zhi")
    size = next_own.shape[0]
    for block in range(own.shape[0] // size):
        rows = pl.ds(block * size, size)
        total = sum_of_blocks(came, own[rows, :], x, rows)
        sent[rows, :] = total.astype(bf16)

        @pl.when(zhi == block)
        def _():
            next_own[...] = total


def elementwise(adapter_of_block, came, own, second, rows):
    columns, units = second.shape
    size = own.shape[0]
    whole = sum_of_blocks(came, own[...], lax.axis_index("zhi"), pl.ds(0, size))
    adapter = adapter_of_block[lax.rem(lax.axis_index("x"), 2)]
    chosen = chosen_columns(adapter, size, columns, columns // 2)
    low = jnp.where(chosen, whole[:, 3 * units :], 0.0).astype(bf16)
    gate = whole[:, :units]
    grad_hidden = whole[:, 2 * units : 3 * units]
    up = whole[:, units : 2 * units] + adapter_scale * product(low, second[...])
    sig = jax.nn.sigmoid(gate)
    act = gate * sig
    hidden = (act * up).astype(bf16)
    grad_up = (grad_hidden * act).astype(bf16)
    grad_gate = (grad_hidden * up * sig * (1.0 + gate * (1.0 - sig))).astype(bf16)
    for copy in range(rows.shape[0]):
        rows[copy, :, :units] = hidden
        rows[copy, :, units : 2 * units] = grad_gate
        rows[copy, :, 2 * units : 3 * units] = grad_up
        rows[copy, :, 3 * units :] = low


def last_products(adapter_of_block, rows, gate, up, down, second, own, other, product_of):
    width, units = gate.shape
    columns = second.shape[0]
    half, quarter = rows.shape[0] // 2, rows.shape[0] // 4
    core = lax.axis_index("core")
    own_start = pl.multiple_of(core * half, half)
    other_start = pl.multiple_of((1 - core) * half, half)

    def put(at, size):
        own[:, at : at + size] = product_of[pl.ds(own_start, half), :size]
        other[:, at : at + size] = product_of[pl.ds(other_start, half), :size]

    grad_up = rows[:, 2 * units : 3 * units]
    value = adapter_scale * trailing_product(grad_up, second[...])
    for block in range(4):
        adapter = adapter_of_block[block % 2]
        part = value[block * quarter : (block + 1) * quarter, :]
        part = jnp.where(chosen_columns(adapter, quarter, columns, columns // 2), part, 0.0)
        product_of[pl.ds(block * quarter, quarter), :columns] = part
    put(2 * width, columns)
    grad_gate = rows[:, units : 2 * units]
    for at in range(0, width, 256):
        product_of[...] = trailing_product(grad_gate, gate[at : at + 256, :]) + trailing_product(
            grad_up, up[at : at + 256, :]
        )
        put(width + at, 256)
    for at in range(0, width, 256):
        product_of[...] = product(rows[:, :units], down[:, at : at + 256])
        put(at, 256)


def core_sum(own, came, sent):
    total = own[...] + came[...]
    peers, rows, _ = sent.shape
    columns = 128
    sums = total.shape[1] - columns
    half = total.shape[0] // 2
    packed = (total[:half, sums:] + total[half:, sums:]).astype(bf16).astype(f32)
    wide = jnp.concatenate(
        [packed[at : at + rows, :] for at in range(0, half, rows)], axis=1
    ).astype(bf16)
    for peer in range(peers):
        sent[peer, :, :sums] = total[peer * rows : (peer + 1) * rows, :sums].astype(bf16)
        sent[peer, :, sums:] = wide


def pipe_sum(came, sums, packed):
    total = came[0].astype(f32)
    for peer in range(1, came.shape[0]):
        total = total + came[peer].astype(f32)
    rows, size = sums.shape
    sums[...] = total[:, :size]
    columns = packed.shape[1]
    packed[...] = jnp.concatenate(
        [total[:, at : at + columns] for at in range(size, total.shape[1], columns)], axis=0
    ).astype(bf16)


def outputs(adapter_of_block, sums, packed, both, first, mixed, grad_tokens, grad_a):
    rows = sums.shape[0]
    columns, width = first.shape
    cores, quarter, _ = packed.shape
    rank = columns // 2
    masks = [
        chosen_columns(adapter_of_block[block], quarter, columns, rank) for block in range(2)
    ]
    core, zlo, y = (lax.axis_index(name) for name in ("core", "zlo", "y"))
    mixed[...] = sums[:, :width].astype(bf16)
    low_own = packed[core, pl.ds(pl.multiple_of(y * rows, rows), rows), :]
    own_mask = chosen_columns(adapter_of_block[zlo], rows, columns, rank)
    low_own = jnp.where(own_mask, low_own.astype(f32), 0.0).astype(bf16)
    grad_tokens[...] = (sums[:, width:] + product(low_own, first[...])).astype(bf16)
    low_back = jnp.concatenate(
        [
            jnp.where(mask, packed[at].astype(f32), 0.0).astype(bf16)
            for at in range(cores)
            for mask in masks
        ],
        axis=0,
    )
    grad_a[...] = leading_product(low_back, both[:, :width])


def on_device(
    tokens,
    gate_weight,
    upward_weight,
    down_weight,
    adapter_first_factors,
    adapter_second_factors,
    adapter_of_block,
    cotangent,
):
    adapters, width, rank = adapter_first_factors.shape
    hidden_units = gate_weight.shape[1]
    columns = adapters * rank
    second = adapter_second_factors.reshape(columns, hidden_units)

    both = jnp.concatenate([tokens, cotangent], axis=1)
    both = lax.all_gather(gather_rows(both, PIPE_LINKS), "core", axis=0, tiled=True)
    row_total = both.shape[0]
    all_columns = 3 * hidden_units + columns

    first_flat = jnp.transpose(adapter_first_factors, (0, 2, 1)).reshape(columns, width)
    sent, own = on_chip(
        first_products,
        [
            jax.ShapeDtypeStruct((row_total, all_columns), bf16),
            jax.ShapeDtypeStruct((row_total // 4, all_columns), f32),
        ],
        [],
        [both, gate_weight, first_flat],
        far=[upward_weight, down_weight],
        scratch=[pltpu.VMEM((row_total, 256), f32), *near_and_done(upward_weight, down_weight)],
    )
    came = lax.all_to_all(sent.reshape(4, row_total // 4, -1), "x", 0, 0)
    sent, own = on_chip(
        middle_sum,
        [
            jax.ShapeDtypeStruct((row_total // 4, all_columns), bf16),
            jax.ShapeDtypeStruct((row_total // 16, all_columns), f32),
        ],
        [],
        [came, own],
    )
    came = lax.all_to_all(sent.reshape(4, row_total // 16, -1), "zhi", 0, 0)
    (rows,) = on_chip(
        elementwise,
        [jax.ShapeDtypeStruct((4, row_total // 16, all_columns), bf16)],
        [adapter_of_block],
        [came, own, second],
    )
    rows = lax.all_to_all(rows, "zhi", 0, 0).reshape(row_total // 4, -1)
    rows = gather_rows(rows, "x")

    own, other = on_chip(
        last_products,
        [jax.ShapeDtypeStruct((row_total // 2, 2 * width + columns), f32)] * 2,
        [adapter_of_block],
        [rows, gate_weight, upward_weight, down_weight, second],
        scratch=[pltpu.VMEM((row_total, 256), f32)],
    )
    came = lax.ppermute(other, "core", [(0, 1), (1, 0)])
    grad_up_all = rows[:, 2 * hidden_units : 3 * hidden_units]
    grad_b = adapter_scale * leading_product(rows[:, 3 * hidden_units :], grad_up_all)
    grad_b = grad_b.reshape(adapters, rank, hidden_units)
    came, grad_b = lax.optimization_barrier((came, grad_b))

    peers = lax.axis_size(PIPE_LINKS)
    (sent,) = on_chip(
        core_sum,
        [jax.ShapeDtypeStruct((peers, row_total // 2 // peers, 4 * width), bf16)],
        [],
        [own, came],
    )
    came = lax.all_to_all(sent, PIPE_LINKS, 0, 0)
    sums, packed = on_chip(
        pipe_sum,
        [
            jax.ShapeDtypeStruct((tokens.shape[0], 2 * width), f32),
            jax.ShapeDtypeStruct((row_total // 4, columns), bf16),
        ],
        [],
        [came],
    )
    packed = lax.all_gather(packed, "core", axis=0)
    mixed, grad_tokens, grad_a = on_chip(
        outputs,
        [
            jax.ShapeDtypeStruct((tokens.shape[0], width), bf16),
            jax.ShapeDtypeStruct((tokens.shape[0], width), bf16),
            jax.ShapeDtypeStruct((columns, width), f32),
        ],
        [adapter_of_block],
        [sums, packed, both, first_flat],
    )
    grad_a = jnp.transpose(grad_a.reshape(adapters, rank, width), (0, 2, 1))
    return mixed, grad_tokens, grad_a, grad_b


def solution(mesh):
    parts = Mesh(mesh.devices.reshape(2, 8, 2, 4, 4), PIPE + TENSOR)
    in_specs = (
        P(PIPE, TENSOR),
        P(TENSOR, PIPE),
        P(TENSOR, PIPE),
        P(PIPE, TENSOR),
        P(None, TENSOR, None),
        P(None, None, PIPE),
        P(),
        P(PIPE, TENSOR),
    )
    out_specs = (
        P(PIPE, TENSOR),
        P(PIPE, TENSOR),
        P(None, TENSOR, None),
        P(None, None, PIPE),
    )
    return jax.shard_map(
        on_device, mesh=parts, in_specs=in_specs, out_specs=out_specs, check_vma=False
    )
```

```python
import jax
import jax.numpy as jnp
from jax import lax
from jax.experimental import pallas as pl
from jax.experimental.pallas import tpu as pltpu
from jax.sharding import Mesh, PartitionSpec as P

PIPE = ("zlo", "y", "core")
TENSOR = ("zhi", "x")
PIPE_LINKS = ("zlo", "y")
adapter_scale = 0.5
sent_scale = 16.0
bf16 = jnp.bfloat16
f32 = jnp.float32


def product(left, right):
    return jnp.dot(left, right, preferred_element_type=f32)


def trailing_product(left, right):
    return lax.dot_general(left, right, (((1,), (1,)), ((), ())), preferred_element_type=f32)


def leading_product(left, right):
    return lax.dot_general(left, right, (((0,), (0,)), ((), ())), preferred_element_type=f32)


def gather_rows(value, axis):
    count = lax.axis_size(axis)
    blocks = jnp.broadcast_to(value[None], (count,) + value.shape)
    return lax.all_to_all(blocks, axis, 0, 0).reshape((count * value.shape[0],) + value.shape[1:])


def own_block(value, first_row, rows):
    return lax.dynamic_slice(
        value, (first_row, 0), (rows, value.shape[1]), allow_negative_indices=False
    )


def on_chip(kernel, out_shape, scalars, arrays, scratch=()):
    return pl.pallas_call(
        kernel,
        out_shape=out_shape,
        in_specs=[pl.BlockSpec(memory_space=pltpu.SMEM)] * len(scalars)
        + [pl.BlockSpec(memory_space=pltpu.VMEM)] * len(arrays),
        out_specs=[pl.BlockSpec(memory_space=pltpu.VMEM)] * len(out_shape),
        scratch_shapes=scratch,
        compiler_params=pltpu.CompilerParams(vmem_limit_bytes=40 * 2**20),
    )(*scalars, *arrays)


def chosen_columns(adapter, rows, columns, rank):
    column = lax.broadcasted_iota(jnp.int32, (rows, columns), 1)
    return (column >= adapter * rank) & (column < (adapter + 1) * rank)


def scatter_sum(value, axis):
    count = lax.axis_size(axis)
    blocks = value.astype(jnp.float16).reshape(count, value.shape[0] // count, -1)
    came = lax.all_to_all(blocks, axis, 0, 0).astype(f32)
    total = came[0]
    for peer in range(1, count):
        total = total + came[peer]
    return total


def elementwise(adapter_of_block, scaled, second, rows):
    columns, units = second.shape
    size = scaled.shape[0]
    whole = scaled[...] * (1 / sent_scale)
    adapter = adapter_of_block[lax.rem(lax.axis_index("x"), 2)]
    chosen = chosen_columns(adapter, size, columns, columns // 2)
    low = jnp.where(chosen, whole[:, 3 * units :], 0.0).astype(bf16)
    gate = whole[:, :units]
    grad_hidden = whole[:, 2 * units : 3 * units]
    up = whole[:, units : 2 * units] + adapter_scale * product(low, second[...])
    sig = jax.nn.sigmoid(gate)
    act = gate * sig
    hidden = (act * up).astype(bf16)
    grad_up = (grad_hidden * act).astype(bf16)
    grad_gate = (grad_hidden * up * sig * (1.0 + gate * (1.0 - sig))).astype(bf16)
    for copy in range(rows.shape[0]):
        rows[copy, :, :units] = hidden
        rows[copy, :, units : 2 * units] = grad_gate
        rows[copy, :, 2 * units : 3 * units] = grad_up
        rows[copy, :, 3 * units :] = low


def last_products(adapter_of_block, rows, gate, up, down, second, own, other, product_of):
    width, units = gate.shape
    columns = second.shape[0]
    half, quarter = rows.shape[0] // 2, rows.shape[0] // 4
    core = lax.axis_index("core")
    own_start = pl.multiple_of(core * half, half)
    other_start = pl.multiple_of((1 - core) * half, half)

    def put(at, size):
        own[:, at : at + size] = product_of[pl.ds(own_start, half), :size]
        other[:, at : at + size] = product_of[pl.ds(other_start, half), :size]

    grad_up = rows[:, 2 * units : 3 * units]
    value = adapter_scale * trailing_product(grad_up, second[...])
    for block in range(4):
        adapter = adapter_of_block[block % 2]
        part = value[block * quarter : (block + 1) * quarter, :]
        part = jnp.where(chosen_columns(adapter, quarter, columns, columns // 2), part, 0.0)
        product_of[pl.ds(block * quarter, quarter), :columns] = part
    put(2 * width, columns)
    grad_gate = rows[:, units : 2 * units]
    for at in range(0, width, 256):
        product_of[...] = trailing_product(grad_gate, gate[at : at + 256, :]) + trailing_product(
            grad_up, up[at : at + 256, :]
        )
        put(width + at, 256)
    for at in range(0, width, 256):
        product_of[...] = product(rows[:, :units], down[:, at : at + 256])
        put(at, 256)


def core_sum(own, came, sent):
    total = own[...] + came[...]
    peers, rows, _ = sent.shape
    columns = 128
    sums = total.shape[1] - columns
    half = total.shape[0] // 2
    packed = (total[:half, sums:] + total[half:, sums:]).astype(bf16).astype(f32)
    wide = jnp.concatenate(
        [packed[at : at + rows, :] for at in range(0, half, rows)], axis=1
    ).astype(bf16)
    for peer in range(peers):
        sent[peer, :, :sums] = total[peer * rows : (peer + 1) * rows, :sums].astype(bf16)
        sent[peer, :, sums:] = wide


def pipe_sum(came, sums, packed):
    total = came[0].astype(f32)
    for peer in range(1, came.shape[0]):
        total = total + came[peer].astype(f32)
    rows, size = sums.shape
    sums[...] = total[:, :size]
    columns = packed.shape[1]
    packed[...] = jnp.concatenate(
        [total[:, at : at + columns] for at in range(size, total.shape[1], columns)], axis=0
    ).astype(bf16)


def outputs(adapter_of_block, sums, packed, both, first, mixed, grad_tokens, grad_a):
    rows = sums.shape[0]
    columns, width = first.shape
    cores, quarter, _ = packed.shape
    rank = columns // 2
    masks = [
        chosen_columns(adapter_of_block[block], quarter, columns, rank) for block in range(2)
    ]
    core, zlo, y = (lax.axis_index(name) for name in ("core", "zlo", "y"))
    mixed[...] = sums[:, :width].astype(bf16)
    low_own = packed[core, pl.ds(pl.multiple_of(y * rows, rows), rows), :]
    own_mask = chosen_columns(adapter_of_block[zlo], rows, columns, rank)
    low_own = jnp.where(own_mask, low_own.astype(f32), 0.0).astype(bf16)
    grad_tokens[...] = (sums[:, width:] + product(low_own, first[...])).astype(bf16)
    low_back = jnp.concatenate(
        [
            jnp.where(mask, packed[at].astype(f32), 0.0).astype(bf16)
            for at in range(cores)
            for mask in masks
        ],
        axis=0,
    )
    grad_a[...] = leading_product(low_back, both[:, :width])


def on_device(
    tokens,
    gate_weight,
    upward_weight,
    down_weight,
    adapter_first_factors,
    adapter_second_factors,
    adapter_of_block,
    cotangent,
):
    adapters, width, rank = adapter_first_factors.shape
    hidden_units = gate_weight.shape[1]
    columns = adapters * rank
    second = adapter_second_factors.reshape(columns, hidden_units)

    both = jnp.concatenate([tokens, cotangent], axis=1)
    both = lax.all_gather(gather_rows(both, PIPE_LINKS), "core", axis=0, tiled=True)
    token_rows, adjoint_rows = both[:, :width], both[:, width:]
    row_total = both.shape[0]
    all_columns = 3 * hidden_units + columns

    first_flat = jnp.transpose(adapter_first_factors, (0, 2, 1)).reshape(columns, width)
    parts = jnp.concatenate(
        [
            (product(token_rows, gate_weight) * sent_scale).astype(jnp.float16),
            (product(token_rows, upward_weight) * sent_scale).astype(jnp.float16),
            (trailing_product(adjoint_rows, down_weight) * sent_scale).astype(jnp.float16),
            (trailing_product(token_rows, first_flat) * sent_scale).astype(jnp.float16),
        ],
        axis=1,
    )
    parts = scatter_sum(scatter_sum(parts, "x"), "zhi")
    (rows,) = on_chip(
        elementwise,
        [jax.ShapeDtypeStruct((4, row_total // 16, all_columns), bf16)],
        [adapter_of_block],
        [parts, second],
    )
    rows = lax.all_to_all(rows, "zhi", 0, 0).reshape(row_total // 4, -1)
    rows = gather_rows(rows, "x")

    own, other = on_chip(
        last_products,
        [jax.ShapeDtypeStruct((row_total // 2, 2 * width + columns), f32)] * 2,
        [adapter_of_block],
        [rows, gate_weight, upward_weight, down_weight, second],
        scratch=[pltpu.VMEM((row_total, 256), f32)],
    )
    came = lax.ppermute(other, "core", [(0, 1), (1, 0)])
    grad_up_all = rows[:, 2 * hidden_units : 3 * hidden_units]
    grad_b = adapter_scale * leading_product(rows[:, 3 * hidden_units :], grad_up_all)
    grad_b = grad_b.reshape(adapters, rank, hidden_units)
    came, grad_b = lax.optimization_barrier((came, grad_b))

    peers = lax.axis_size(PIPE_LINKS)
    (sent,) = on_chip(
        core_sum,
        [jax.ShapeDtypeStruct((peers, row_total // 2 // peers, 4 * width), bf16)],
        [],
        [own, came],
    )
    came = lax.all_to_all(sent, PIPE_LINKS, 0, 0)
    sums, packed = on_chip(
        pipe_sum,
        [
            jax.ShapeDtypeStruct((tokens.shape[0], 2 * width), f32),
            jax.ShapeDtypeStruct((row_total // 4, columns), bf16),
        ],
        [],
        [came],
    )
    packed = lax.all_gather(packed, "core", axis=0)
    mixed, grad_tokens, grad_a = on_chip(
        outputs,
        [
            jax.ShapeDtypeStruct((tokens.shape[0], width), bf16),
            jax.ShapeDtypeStruct((tokens.shape[0], width), bf16),
            jax.ShapeDtypeStruct((columns, width), f32),
        ],
        [adapter_of_block],
        [sums, packed, both, first_flat],
    )
    grad_a = jnp.transpose(grad_a.reshape(adapters, rank, width), (0, 2, 1))
    return mixed, grad_tokens, grad_a, grad_b


def solution(mesh):
    parts = Mesh(mesh.devices.reshape(2, 8, 2, 4, 4), PIPE + TENSOR)
    in_specs = (
        P(PIPE, TENSOR),
        P(TENSOR, PIPE),
        P(TENSOR, PIPE),
        P(PIPE, TENSOR),
        P(None, TENSOR, None),
        P(None, None, PIPE),
        P(),
        P(PIPE, TENSOR),
    )
    out_specs = (
        P(PIPE, TENSOR),
        P(PIPE, TENSOR),
        P(None, TENSOR, None),
        P(None, None, PIPE),
    )
    return jax.shard_map(
        on_device, mesh=parts, in_specs=in_specs, out_specs=out_specs, check_vma=False
    )
```

```python
import jax
import jax.numpy as jnp
from jax import lax
from jax.experimental import pallas as pl
from jax.experimental.pallas import tpu as pltpu
from jax.sharding import Mesh, PartitionSpec as P

PIPE = ("zlo", "y", "core")
TENSOR = ("zhi", "x")
PIPE_LINKS = ("zlo", "y")
adapter_scale = 0.5
sent_scale = 16.0
bf16 = jnp.bfloat16
f32 = jnp.float32


def product(left, right):
    return jnp.dot(left, right, preferred_element_type=f32)


def trailing_product(left, right):
    return lax.dot_general(left, right, (((1,), (1,)), ((), ())), preferred_element_type=f32)


def leading_product(left, right):
    return lax.dot_general(left, right, (((0,), (0,)), ((), ())), preferred_element_type=f32)


def gather_rows(value, axis):
    count = lax.axis_size(axis)
    blocks = jnp.broadcast_to(value[None], (count,) + value.shape)
    return lax.all_to_all(blocks, axis, 0, 0).reshape((count * value.shape[0],) + value.shape[1:])


def own_block(value, first_row, rows):
    return lax.dynamic_slice(
        value, (first_row, 0), (rows, value.shape[1]), allow_negative_indices=False
    )


def on_chip(kernel, out_shape, scalars, arrays, scratch=()):
    return pl.pallas_call(
        kernel,
        out_shape=out_shape,
        in_specs=[pl.BlockSpec(memory_space=pltpu.SMEM)] * len(scalars)
        + [pl.BlockSpec(memory_space=pltpu.VMEM)] * len(arrays),
        out_specs=[pl.BlockSpec(memory_space=pltpu.VMEM)] * len(out_shape),
        scratch_shapes=scratch,
        compiler_params=pltpu.CompilerParams(vmem_limit_bytes=40 * 2**20),
    )(*scalars, *arrays)


def chosen_columns(adapter, rows, columns, rank):
    column = lax.broadcasted_iota(jnp.int32, (rows, columns), 1)
    return (column >= adapter * rank) & (column < (adapter + 1) * rank)


def scatter_sum(value, axis):
    count = lax.axis_size(axis)
    blocks = value.astype(jnp.float16).reshape(count, value.shape[0] // count, -1)
    return jnp.sum(lax.all_to_all(blocks, axis, 0, 0).astype(f32), axis=0)


def elementwise(adapter_of_block, scaled, second, rows):
    columns, units = second.shape
    size = scaled.shape[0]
    whole = scaled[...] * (1 / sent_scale)
    adapter = adapter_of_block[lax.rem(lax.axis_index("x"), 2)]
    chosen = chosen_columns(adapter, size, columns, columns // 2)
    low = jnp.where(chosen, whole[:, 3 * units :], 0.0).astype(bf16)
    gate = whole[:, :units]
    grad_hidden = whole[:, 2 * units : 3 * units]
    up = whole[:, units : 2 * units] + adapter_scale * product(low, second[...])
    sig = jax.nn.sigmoid(gate)
    act = gate * sig
    hidden = (act * up).astype(bf16)
    grad_up = (grad_hidden * act).astype(bf16)
    grad_gate = (grad_hidden * up * sig * (1.0 + gate * (1.0 - sig))).astype(bf16)
    for copy in range(rows.shape[0]):
        rows[copy, :, :units] = hidden
        rows[copy, :, units : 2 * units] = grad_gate
        rows[copy, :, 2 * units : 3 * units] = grad_up
        rows[copy, :, 3 * units :] = low


def last_products(adapter_of_block, rows, gate, up, down, second, own, other, product_of):
    width, units = gate.shape
    columns = second.shape[0]
    half, quarter = rows.shape[0] // 2, rows.shape[0] // 4
    core = lax.axis_index("core")
    own_start = pl.multiple_of(core * half, half)
    other_start = pl.multiple_of((1 - core) * half, half)

    def put(at, size):
        own[:, at : at + size] = product_of[pl.ds(own_start, half), :size]
        other[:, at : at + size] = product_of[pl.ds(other_start, half), :size].astype(bf16)

    grad_up = rows[:, 2 * units : 3 * units]
    value = adapter_scale * trailing_product(grad_up, second[...])
    for block in range(4):
        adapter = adapter_of_block[block % 2]
        part = value[block * quarter : (block + 1) * quarter, :]
        part = jnp.where(chosen_columns(adapter, quarter, columns, columns // 2), part, 0.0)
        product_of[pl.ds(block * quarter, quarter), :columns] = part
    put(2 * width, columns)
    grad_gate = rows[:, units : 2 * units]
    for at in range(0, width, 256):
        product_of[...] = trailing_product(grad_gate, gate[at : at + 256, :]) + trailing_product(
            grad_up, up[at : at + 256, :]
        )
        put(width + at, 256)
    for at in range(0, width, 256):
        product_of[...] = product(rows[:, :units], down[:, at : at + 256])
        put(at, 256)


def core_sum(own, came, sent):
    total = own[...] + came[...].astype(f32)
    peers, rows, _ = sent.shape
    columns = 128
    sums = total.shape[1] - columns
    half = total.shape[0] // 2
    packed = (total[:half, sums:] + total[half:, sums:]).astype(bf16).astype(f32)
    wide = jnp.concatenate(
        [packed[at : at + rows, :] for at in range(0, half, rows)], axis=1
    ).astype(bf16)
    for peer in range(peers):
        sent[peer, :, :sums] = total[peer * rows : (peer + 1) * rows, :sums].astype(bf16)
        sent[peer, :, sums:] = wide


def pipe_sum(came, sums, packed):
    total = came[0].astype(f32)
    for peer in range(1, came.shape[0]):
        total = total + came[peer].astype(f32)
    rows, size = sums.shape
    sums[...] = total[:, :size]
    columns = packed.shape[1]
    packed[...] = jnp.concatenate(
        [total[:, at : at + columns] for at in range(size, total.shape[1], columns)], axis=0
    ).astype(bf16)


def outputs(adapter_of_block, sums, packed, both, first, mixed, grad_tokens, grad_a):
    rows = sums.shape[0]
    columns, width = first.shape
    cores, quarter, _ = packed.shape
    rank = columns // 2
    masks = [
        chosen_columns(adapter_of_block[block], quarter, columns, rank) for block in range(2)
    ]
    core, zlo, y = (lax.axis_index(name) for name in ("core", "zlo", "y"))
    mixed[...] = sums[:, :width].astype(bf16)
    low_own = packed[core, pl.ds(pl.multiple_of(y * rows, rows), rows), :]
    own_mask = chosen_columns(adapter_of_block[zlo], rows, columns, rank)
    low_own = jnp.where(own_mask, low_own.astype(f32), 0.0).astype(bf16)
    grad_tokens[...] = (sums[:, width:] + product(low_own, first[...])).astype(bf16)
    low_back = jnp.concatenate(
        [
            jnp.where(mask, packed[at].astype(f32), 0.0).astype(bf16)
            for at in range(cores)
            for mask in masks
        ],
        axis=0,
    )
    grad_a[...] = leading_product(low_back, both[:, :width])


def on_device(
    tokens,
    gate_weight,
    upward_weight,
    down_weight,
    adapter_first_factors,
    adapter_second_factors,
    adapter_of_block,
    cotangent,
):
    adapters, width, rank = adapter_first_factors.shape
    hidden_units = gate_weight.shape[1]
    columns = adapters * rank
    second = adapter_second_factors.reshape(columns, hidden_units)

    both = jnp.concatenate([tokens, cotangent], axis=1)
    both = lax.all_gather(gather_rows(both, PIPE_LINKS), "core", axis=0, tiled=True)
    token_rows, adjoint_rows = both[:, :width], both[:, width:]
    row_total = both.shape[0]
    all_columns = 3 * hidden_units + columns

    first_flat = jnp.transpose(adapter_first_factors, (0, 2, 1)).reshape(columns, width)
    parts = jnp.concatenate(
        [
            (product(token_rows, gate_weight) * sent_scale).astype(jnp.float16),
            (product(token_rows, upward_weight) * sent_scale).astype(jnp.float16),
            (trailing_product(adjoint_rows, down_weight) * sent_scale).astype(jnp.float16),
            (trailing_product(token_rows, first_flat) * sent_scale).astype(jnp.float16),
        ],
        axis=1,
    )
    parts = scatter_sum(scatter_sum(parts, "x"), "zhi")
    (rows,) = on_chip(
        elementwise,
        [jax.ShapeDtypeStruct((4, row_total // 16, all_columns), bf16)],
        [adapter_of_block],
        [parts, second],
    )
    rows = lax.all_to_all(rows, "zhi", 0, 0).reshape(row_total // 4, -1)
    rows = gather_rows(rows, "x")

    own, other = on_chip(
        last_products,
        [
            jax.ShapeDtypeStruct((row_total // 2, 2 * width + columns), kind)
            for kind in (f32, bf16)
        ],
        [adapter_of_block],
        [rows, gate_weight, upward_weight, down_weight, second],
        scratch=[pltpu.VMEM((row_total, 256), f32)],
    )
    came = lax.ppermute(other, "core", [(0, 1), (1, 0)])
    grad_up_all = rows[:, 2 * hidden_units : 3 * hidden_units]
    grad_b = adapter_scale * leading_product(rows[:, 3 * hidden_units :], grad_up_all)
    grad_b = grad_b.reshape(adapters, rank, hidden_units)
    came, grad_b = lax.optimization_barrier((came, grad_b))

    peers = lax.axis_size(PIPE_LINKS)
    (sent,) = on_chip(
        core_sum,
        [jax.ShapeDtypeStruct((peers, row_total // 2 // peers, 4 * width), bf16)],
        [],
        [own, came],
    )
    came = lax.all_to_all(sent, PIPE_LINKS, 0, 0)
    sums, packed = on_chip(
        pipe_sum,
        [
            jax.ShapeDtypeStruct((tokens.shape[0], 2 * width), f32),
            jax.ShapeDtypeStruct((row_total // 4, columns), bf16),
        ],
        [],
        [came],
    )
    packed = lax.all_gather(packed, "core", axis=0)
    mixed, grad_tokens, grad_a = on_chip(
        outputs,
        [
            jax.ShapeDtypeStruct((tokens.shape[0], width), bf16),
            jax.ShapeDtypeStruct((tokens.shape[0], width), bf16),
            jax.ShapeDtypeStruct((columns, width), f32),
        ],
        [adapter_of_block],
        [sums, packed, both, first_flat],
    )
    grad_a = jnp.transpose(grad_a.reshape(adapters, rank, width), (0, 2, 1))
    return mixed, grad_tokens, grad_a, grad_b


def solution(mesh):
    parts = Mesh(mesh.devices.reshape(2, 8, 2, 4, 4), PIPE + TENSOR)
    in_specs = (
        P(PIPE, TENSOR),
        P(TENSOR, PIPE),
        P(TENSOR, PIPE),
        P(PIPE, TENSOR),
        P(None, TENSOR, None),
        P(None, None, PIPE),
        P(),
        P(PIPE, TENSOR),
    )
    out_specs = (
        P(PIPE, TENSOR),
        P(PIPE, TENSOR),
        P(None, TENSOR, None),
        P(None, None, PIPE),
    )
    return jax.shard_map(
        on_device, mesh=parts, in_specs=in_specs, out_specs=out_specs, check_vma=False
    )
```

```python
import jax
import jax.numpy as jnp
from jax import lax
from jax.experimental import pallas as pl
from jax.experimental.pallas import tpu as pltpu
from jax.sharding import Mesh, PartitionSpec as P

PIPE = ("zlo", "y", "core")
TENSOR = ("zhi", "x")
PIPE_LINKS = ("zlo", "y")
adapter_scale = 0.5
sent_scale = 64.0
bf16 = jnp.bfloat16
f32 = jnp.float32


def product(left, right):
    return jnp.dot(left, right, preferred_element_type=f32)


def trailing_product(left, right):
    return lax.dot_general(left, right, (((1,), (1,)), ((), ())), preferred_element_type=f32)


def leading_product(left, right):
    return lax.dot_general(left, right, (((0,), (0,)), ((), ())), preferred_element_type=f32)


def gather_rows(value, axis):
    count = lax.axis_size(axis)
    blocks = jnp.broadcast_to(value[None], (count,) + value.shape)
    return lax.all_to_all(blocks, axis, 0, 0).reshape((count * value.shape[0],) + value.shape[1:])


def own_block(value, first_row, rows):
    return lax.dynamic_slice(
        value, (first_row, 0), (rows, value.shape[1]), allow_negative_indices=False
    )


def on_chip(kernel, out_shape, scalars, arrays):
    return pl.pallas_call(
        kernel,
        out_shape=out_shape,
        in_specs=[pl.BlockSpec(memory_space=pltpu.SMEM)] * len(scalars)
        + [pl.BlockSpec(memory_space=pltpu.VMEM)] * len(arrays),
        out_specs=[pl.BlockSpec(memory_space=pltpu.VMEM)] * len(out_shape),
        compiler_params=pltpu.CompilerParams(vmem_limit_bytes=40 * 2**20),
    )(*scalars, *arrays)


def chosen_columns(adapter, rows, columns, rank):
    column = lax.broadcasted_iota(jnp.int32, (rows, columns), 1)
    return (column >= adapter * rank) & (column < (adapter + 1) * rank)


def scatter_sum(value, axis):
    count = lax.axis_size(axis)
    blocks = value.astype(jnp.float16).reshape(count, value.shape[0] // count, -1)
    return jnp.sum(lax.all_to_all(blocks, axis, 0, 0).astype(f32), axis=0)


def elementwise(adapter_of_block, scaled, second, rows):
    columns, units = second.shape
    size = scaled.shape[0]
    whole = scaled[...] * (1 / sent_scale)
    adapter = adapter_of_block[lax.rem(lax.axis_index("x"), 2)]
    chosen = chosen_columns(adapter, size, columns, columns // 2)
    low = jnp.where(chosen, whole[:, 3 * units :], 0.0).astype(bf16)
    gate = whole[:, :units]
    grad_hidden = whole[:, 2 * units : 3 * units]
    up = whole[:, units : 2 * units] + adapter_scale * product(low, second[...])
    sig = jax.nn.sigmoid(gate)
    act = gate * sig
    hidden = (act * up).astype(bf16)
    grad_up = (grad_hidden * act).astype(bf16)
    grad_gate = (grad_hidden * up * sig * (1.0 + gate * (1.0 - sig))).astype(bf16)
    for copy in range(rows.shape[0]):
        rows[copy, :, :units] = hidden
        rows[copy, :, units : 2 * units] = grad_gate
        rows[copy, :, 2 * units : 3 * units] = grad_up
        rows[copy, :, 3 * units :] = low


def last_products(adapter_of_block, rows, gate, up, down, second, own, other):
    width, units = gate.shape
    columns = second.shape[0]
    half, quarter = rows.shape[0] // 2, rows.shape[0] // 4
    is_first = lax.axis_index("core") == 0

    def put(value, at):
        low_half, high_half = value[:half], value[half:]
        columns_at = slice(at, at + value.shape[1])
        own[:, columns_at] = jnp.where(is_first, low_half, high_half)
        other[:, columns_at] = jnp.where(is_first, high_half, low_half).astype(bf16)

    grad_up = rows[:, 2 * units : 3 * units]
    value = adapter_scale * trailing_product(grad_up, second[...])
    masks = [
        chosen_columns(adapter_of_block[block % 2], quarter, columns, columns // 2)
        for block in range(4)
    ]
    put(jnp.where(jnp.concatenate(masks, axis=0), value, 0.0), 2 * width)
    grad_gate = rows[:, units : 2 * units]
    for at in range(0, width, 256):
        value = trailing_product(grad_gate, gate[at : at + 256, :])
        put(value + trailing_product(grad_up, up[at : at + 256, :]), width + at)
    for at in range(0, width, 256):
        put(product(rows[:, :units], down[:, at : at + 256]), at)


def core_sum(own, came, sent):
    total = own[...] + came[...].astype(f32)
    peers, rows, _ = sent.shape
    columns = 128
    sums = total.shape[1] - columns
    half = total.shape[0] // 2
    packed = (total[:half, sums:] + total[half:, sums:]).astype(bf16).astype(f32)
    wide = jnp.concatenate(
        [packed[at : at + rows, :] for at in range(0, half, rows)], axis=1
    ).astype(bf16)
    for peer in range(peers):
        sent[peer, :, :sums] = total[peer * rows : (peer + 1) * rows, :sums].astype(bf16)
        sent[peer, :, sums:] = wide


def pipe_sum(came, sums, packed):
    total = came[0].astype(f32)
    for peer in range(1, came.shape[0]):
        total = total + came[peer].astype(f32)
    rows, size = sums.shape
    sums[...] = total[:, :size]
    columns = packed.shape[1]
    packed[...] = jnp.concatenate(
        [total[:, at : at + columns] for at in range(size, total.shape[1], columns)], axis=0
    ).astype(bf16)


def outputs(adapter_of_block, sums, packed, both, first, mixed, grad_tokens, grad_a):
    rows = sums.shape[0]
    columns, width = first.shape
    cores, quarter, _ = packed.shape
    rank = columns // 2
    masks = [
        chosen_columns(adapter_of_block[block], quarter, columns, rank) for block in range(2)
    ]
    core, zlo, y = (lax.axis_index(name) for name in ("core", "zlo", "y"))
    mixed[...] = sums[:, :width].astype(bf16)
    low_own = packed[core, pl.ds(pl.multiple_of(y * rows, rows), rows), :]
    own_mask = chosen_columns(adapter_of_block[zlo], rows, columns, rank)
    low_own = jnp.where(own_mask, low_own.astype(f32), 0.0).astype(bf16)
    grad_tokens[...] = (sums[:, width:] + product(low_own, first[...])).astype(bf16)
    low_back = jnp.concatenate(
        [
            jnp.where(mask, packed[at].astype(f32), 0.0).astype(bf16)
            for at in range(cores)
            for mask in masks
        ],
        axis=0,
    )
    grad_a[...] = leading_product(low_back, both[:, :width])


def on_device(
    tokens,
    gate_weight,
    upward_weight,
    down_weight,
    adapter_first_factors,
    adapter_second_factors,
    adapter_of_block,
    cotangent,
):
    adapters, width, rank = adapter_first_factors.shape
    hidden_units = gate_weight.shape[1]
    columns = adapters * rank
    second = adapter_second_factors.reshape(columns, hidden_units)

    both = jnp.concatenate([tokens, cotangent], axis=1)
    both = lax.all_gather(gather_rows(both, PIPE_LINKS), "core", axis=0, tiled=True)
    token_rows, adjoint_rows = both[:, :width], both[:, width:]
    row_total = both.shape[0]
    all_columns = 3 * hidden_units + columns

    first_flat = jnp.transpose(adapter_first_factors, (0, 2, 1)).reshape(columns, width)
    parts = jnp.concatenate(
        [
            (product(token_rows, gate_weight) * sent_scale).astype(jnp.float16),
            (product(token_rows, upward_weight) * sent_scale).astype(jnp.float16),
            (trailing_product(adjoint_rows, down_weight) * sent_scale).astype(jnp.float16),
            (trailing_product(token_rows, first_flat) * sent_scale).astype(jnp.float16),
        ],
        axis=1,
    )
    parts = scatter_sum(scatter_sum(parts, "x"), "zhi")
    (rows,) = on_chip(
        elementwise,
        [jax.ShapeDtypeStruct((4, row_total // 16, all_columns), bf16)],
        [adapter_of_block],
        [parts, second],
    )
    rows = lax.all_to_all(rows, "zhi", 0, 0).reshape(row_total // 4, -1)
    rows = gather_rows(rows, "x")

    own, other = on_chip(
        last_products,
        [
            jax.ShapeDtypeStruct((row_total // 2, 2 * width + columns), kind)
            for kind in (f32, bf16)
        ],
        [adapter_of_block],
        [rows, gate_weight, upward_weight, down_weight, second],
    )
    came = lax.ppermute(other, "core", [(0, 1), (1, 0)])
    grad_up_all = rows[:, 2 * hidden_units : 3 * hidden_units]
    grad_b = adapter_scale * leading_product(rows[:, 3 * hidden_units :], grad_up_all)
    grad_b = grad_b.reshape(adapters, rank, hidden_units)
    came, grad_b = lax.optimization_barrier((came, grad_b))

    peers = lax.axis_size(PIPE_LINKS)
    (sent,) = on_chip(
        core_sum,
        [jax.ShapeDtypeStruct((peers, row_total // 2 // peers, 4 * width), bf16)],
        [],
        [own, came],
    )
    came = lax.all_to_all(sent, PIPE_LINKS, 0, 0)
    sums, packed = on_chip(
        pipe_sum,
        [
            jax.ShapeDtypeStruct((tokens.shape[0], 2 * width), f32),
            jax.ShapeDtypeStruct((row_total // 4, columns), bf16),
        ],
        [],
        [came],
    )
    packed = lax.all_gather(packed, "core", axis=0)
    mixed, grad_tokens, grad_a = on_chip(
        outputs,
        [
            jax.ShapeDtypeStruct((tokens.shape[0], width), bf16),
            jax.ShapeDtypeStruct((tokens.shape[0], width), bf16),
            jax.ShapeDtypeStruct((columns, width), f32),
        ],
        [adapter_of_block],
        [sums, packed, both, first_flat],
    )
    grad_a = jnp.transpose(grad_a.reshape(adapters, rank, width), (0, 2, 1))
    return mixed, grad_tokens, grad_a, grad_b


def solution(mesh):
    parts = Mesh(mesh.devices.reshape(2, 8, 2, 4, 4), PIPE + TENSOR)
    in_specs = (
        P(PIPE, TENSOR),
        P(TENSOR, PIPE),
        P(TENSOR, PIPE),
        P(PIPE, TENSOR),
        P(None, TENSOR, None),
        P(None, None, PIPE),
        P(),
        P(PIPE, TENSOR),
    )
    out_specs = (
        P(PIPE, TENSOR),
        P(PIPE, TENSOR),
        P(None, TENSOR, None),
        P(None, None, PIPE),
    )
    return jax.shard_map(
        on_device, mesh=parts, in_specs=in_specs, out_specs=out_specs, check_vma=False
    )
```

```python
import jax
import jax.numpy as jnp
from jax import lax
from jax.experimental import pallas as pl
from jax.experimental.pallas import tpu as pltpu
from jax.sharding import Mesh, PartitionSpec as P

PIPE = ("zlo", "y", "core")
TENSOR = ("zhi", "x")
PIPE_LINKS = ("zlo", "y")
adapter_scale = 0.5
sent_scale = 64.0
bf16 = jnp.bfloat16
f32 = jnp.float32


def product(left, right):
    return jnp.dot(left, right, preferred_element_type=f32)


def trailing_product(left, right):
    return lax.dot_general(left, right, (((1,), (1,)), ((), ())), preferred_element_type=f32)


def leading_product(left, right):
    return lax.dot_general(left, right, (((0,), (0,)), ((), ())), preferred_element_type=f32)


def gather_rows(value, axis):
    count = lax.axis_size(axis)
    blocks = jnp.broadcast_to(value[None], (count,) + value.shape)
    return lax.all_to_all(blocks, axis, 0, 0).reshape((count * value.shape[0],) + value.shape[1:])


def own_block(value, first_row, rows):
    return lax.dynamic_slice(
        value, (first_row, 0), (rows, value.shape[1]), allow_negative_indices=False
    )


def on_chip(kernel, out_shape, scalars, arrays):
    return pl.pallas_call(
        kernel,
        out_shape=out_shape,
        in_specs=[pl.BlockSpec(memory_space=pltpu.SMEM)] * len(scalars)
        + [pl.BlockSpec(memory_space=pltpu.VMEM)] * len(arrays),
        out_specs=[pl.BlockSpec(memory_space=pltpu.VMEM)] * len(out_shape),
        compiler_params=pltpu.CompilerParams(vmem_limit_bytes=40 * 2**20),
    )(*scalars, *arrays)


def chosen_columns(adapter, rows, columns, rank):
    column = lax.broadcasted_iota(jnp.int32, (rows, columns), 1)
    return (column >= adapter * rank) & (column < (adapter + 1) * rank)


def scatter_sum(value, axis):
    count = lax.axis_size(axis)
    blocks = value.astype(jnp.float16).reshape(count, value.shape[0] // count, -1)
    return jnp.sum(lax.all_to_all(blocks, axis, 0, 0).astype(f32), axis=0)


def elementwise(adapter_of_block, scaled, second, rows):
    columns, units = second.shape
    size = scaled.shape[0]
    whole = scaled[...] * (1 / sent_scale)
    adapter = adapter_of_block[lax.rem(lax.axis_index("x"), 2)]
    chosen = chosen_columns(adapter, size, columns, columns // 2)
    low = jnp.where(chosen, whole[:, 3 * units :], 0.0).astype(bf16)
    gate = whole[:, :units]
    grad_hidden = whole[:, 2 * units : 3 * units]
    up = whole[:, units : 2 * units] + adapter_scale * product(low, second[...])
    sig = jax.nn.sigmoid(gate)
    act = gate * sig
    hidden = (act * up).astype(bf16)
    grad_up = (grad_hidden * act).astype(bf16)
    grad_gate = (grad_hidden * up * sig * (1.0 + gate * (1.0 - sig))).astype(bf16)
    for copy in range(rows.shape[0]):
        rows[copy, :, :units] = hidden
        rows[copy, :, units : 2 * units] = grad_gate
        rows[copy, :, 2 * units : 3 * units] = grad_up
        rows[copy, :, 3 * units :] = low


def last_products(adapter_of_block, rows, gate, up, down, second, own, other):
    width, units = gate.shape
    columns = second.shape[0]
    half, quarter = rows.shape[0] // 2, rows.shape[0] // 4
    is_first = lax.axis_index("core") == 0

    def put(value, at):
        low_half, high_half = value[:half], value[half:]
        columns_at = slice(at, at + value.shape[1])
        own[:, columns_at] = jnp.where(is_first, low_half, high_half)
        other[:, columns_at] = jnp.where(is_first, high_half, low_half).astype(bf16)

    grad_up = rows[:, 2 * units : 3 * units]
    value = adapter_scale * trailing_product(grad_up, second[...])
    masks = [
        chosen_columns(adapter_of_block[block % 2], quarter, columns, columns // 2)
        for block in range(4)
    ]
    put(jnp.where(jnp.concatenate(masks, axis=0), value, 0.0), 2 * width)
    grad_gate = rows[:, units : 2 * units]
    for at in range(0, width, 512):
        value = trailing_product(grad_gate, gate[at : at + 512, :])
        put(value + trailing_product(grad_up, up[at : at + 512, :]), width + at)
    for at in range(0, width, 512):
        put(product(rows[:, :units], down[:, at : at + 512]), at)


def core_sum(own, came, sent):
    total = own[...] + came[...].astype(f32)
    peers, rows, _ = sent.shape
    columns = 128
    sums = total.shape[1] - columns
    half = total.shape[0] // 2
    packed = (total[:half, sums:] + total[half:, sums:]).astype(bf16).astype(f32)
    wide = jnp.concatenate(
        [packed[at : at + rows, :] for at in range(0, half, rows)], axis=1
    ).astype(bf16)
    for peer in range(peers):
        sent[peer, :, :sums] = total[peer * rows : (peer + 1) * rows, :sums].astype(bf16)
        sent[peer, :, sums:] = wide


def pipe_sum(came, sums, packed):
    total = came[0].astype(f32)
    for peer in range(1, came.shape[0]):
        total = total + came[peer].astype(f32)
    rows, size = sums.shape
    sums[...] = total[:, :size]
    columns = packed.shape[1]
    packed[...] = jnp.concatenate(
        [total[:, at : at + columns] for at in range(size, total.shape[1], columns)], axis=0
    ).astype(bf16)


def outputs(
    adapter_of_block,
    sums,
    packed,
    both,
    first,
    mixed_far,
    grad_tokens_far,
    grad_a_far,
    mixed,
    grad_tokens,
    grad_a,
    done,
):
    rows = sums.shape[0]
    columns, width = first.shape
    cores, quarter, _ = packed.shape
    rank = columns // 2
    masks = [
        chosen_columns(adapter_of_block[block], quarter, columns, rank) for block in range(2)
    ]
    low_back = jnp.concatenate(
        [
            jnp.where(mask, packed[at].astype(f32), 0.0).astype(bf16)
            for at in range(cores)
            for mask in masks
        ],
        axis=0,
    )
    grad_a[...] = leading_product(low_back, both[:, :width])
    write_grad_a = pltpu.make_async_copy(grad_a, grad_a_far, done.at[0])
    write_grad_a.start()
    mixed[...] = sums[:, :width].astype(bf16)
    write_mixed = pltpu.make_async_copy(mixed, mixed_far, done.at[1])
    write_mixed.start()
    core, zlo, y = (lax.axis_index(name) for name in ("core", "zlo", "y"))
    low_own = packed[core, pl.ds(pl.multiple_of(y * rows, rows), rows), :]
    own_mask = chosen_columns(adapter_of_block[zlo], rows, columns, rank)
    low_own = jnp.where(own_mask, low_own.astype(f32), 0.0).astype(bf16)
    grad_tokens[...] = (sums[:, width:] + product(low_own, first[...])).astype(bf16)
    write_grad_tokens = pltpu.make_async_copy(grad_tokens, grad_tokens_far, done.at[2])
    write_grad_tokens.start()
    write_grad_a.wait()
    write_mixed.wait()
    write_grad_tokens.wait()


def on_device(
    tokens,
    gate_weight,
    upward_weight,
    down_weight,
    adapter_first_factors,
    adapter_second_factors,
    adapter_of_block,
    cotangent,
):
    adapters, width, rank = adapter_first_factors.shape
    hidden_units = gate_weight.shape[1]
    columns = adapters * rank
    second = adapter_second_factors.reshape(columns, hidden_units)

    both = jnp.concatenate([tokens, cotangent], axis=1)
    both = lax.all_gather(gather_rows(both, PIPE_LINKS), "core", axis=0, tiled=True)
    token_rows, adjoint_rows = both[:, :width], both[:, width:]
    row_total = both.shape[0]
    all_columns = 3 * hidden_units + columns

    first_flat = jnp.transpose(adapter_first_factors, (0, 2, 1)).reshape(columns, width)
    parts = jnp.concatenate(
        [
            (product(token_rows, gate_weight) * sent_scale).astype(jnp.float16),
            (product(token_rows, upward_weight) * sent_scale).astype(jnp.float16),
            (trailing_product(adjoint_rows, down_weight) * sent_scale).astype(jnp.float16),
            (trailing_product(token_rows, first_flat) * sent_scale).astype(jnp.float16),
        ],
        axis=1,
    )
    parts = scatter_sum(scatter_sum(parts, "x"), "zhi")
    (rows,) = on_chip(
        elementwise,
        [jax.ShapeDtypeStruct((4, row_total // 16, all_columns), bf16)],
        [adapter_of_block],
        [parts, second],
    )
    rows = lax.all_to_all(rows, "zhi", 0, 0).reshape(row_total // 4, -1)
    rows = gather_rows(rows, "x")

    own, other = on_chip(
        last_products,
        [
            jax.ShapeDtypeStruct((row_total // 2, 2 * width + columns), kind)
            for kind in (f32, bf16)
        ],
        [adapter_of_block],
        [rows, gate_weight, upward_weight, down_weight, second],
    )
    came = lax.ppermute(other, "core", [(0, 1), (1, 0)])
    grad_up_all = rows[:, 2 * hidden_units : 3 * hidden_units]
    grad_b = adapter_scale * leading_product(rows[:, 3 * hidden_units :], grad_up_all)
    grad_b = grad_b.reshape(adapters, rank, hidden_units)
    came, grad_b = lax.optimization_barrier((came, grad_b))

    peers = lax.axis_size(PIPE_LINKS)
    (sent,) = on_chip(
        core_sum,
        [jax.ShapeDtypeStruct((peers, row_total // 2 // peers, 4 * width), bf16)],
        [],
        [own, came],
    )
    came = lax.all_to_all(sent, PIPE_LINKS, 0, 0)
    sums, packed = on_chip(
        pipe_sum,
        [
            jax.ShapeDtypeStruct((tokens.shape[0], 2 * width), f32),
            jax.ShapeDtypeStruct((row_total // 4, columns), bf16),
        ],
        [],
        [came],
    )
    packed = lax.all_gather(packed, "core", axis=0)
    results = [
        jax.ShapeDtypeStruct((tokens.shape[0], width), bf16),
        jax.ShapeDtypeStruct((tokens.shape[0], width), bf16),
        jax.ShapeDtypeStruct((columns, width), f32),
    ]
    mixed, grad_tokens, grad_a = pl.pallas_call(
        outputs,
        out_shape=results,
        in_specs=[pl.BlockSpec(memory_space=pltpu.SMEM)]
        + [pl.BlockSpec(memory_space=pltpu.VMEM)] * 4,
        out_specs=[pl.BlockSpec(memory_space=pl.ANY)] * 3,
        scratch_shapes=[pltpu.VMEM(result.shape, result.dtype) for result in results]
        + [pltpu.SemaphoreType.DMA((3,))],
    )(adapter_of_block, sums, packed, both, first_flat)
    grad_a = jnp.transpose(grad_a.reshape(adapters, rank, width), (0, 2, 1))
    return mixed, grad_tokens, grad_a, grad_b


def solution(mesh):
    parts = Mesh(mesh.devices.reshape(2, 8, 2, 4, 4), PIPE + TENSOR)
    in_specs = (
        P(PIPE, TENSOR),
        P(TENSOR, PIPE),
        P(TENSOR, PIPE),
        P(PIPE, TENSOR),
        P(None, TENSOR, None),
        P(None, None, PIPE),
        P(),
        P(PIPE, TENSOR),
    )
    out_specs = (
        P(PIPE, TENSOR),
        P(PIPE, TENSOR),
        P(None, TENSOR, None),
        P(None, None, PIPE),
    )
    return jax.shard_map(
        on_device, mesh=parts, in_specs=in_specs, out_specs=out_specs, check_vma=False
    )
```

```python
import jax
import jax.numpy as jnp
from jax import lax
from jax.experimental import pallas as pl
from jax.experimental.pallas import tpu as pltpu
from jax.sharding import Mesh, PartitionSpec as P

PIPE = ("zlo", "y", "core")
TENSOR = ("zhi", "x")
PIPE_LINKS = ("zlo", "y")
adapter_scale = 0.5
sent_scale = 64.0
bf16 = jnp.bfloat16
f32 = jnp.float32


def product(left, right):
    return jnp.dot(left, right, preferred_element_type=f32)


def trailing_product(left, right):
    return lax.dot_general(left, right, (((1,), (1,)), ((), ())), preferred_element_type=f32)


def leading_product(left, right):
    return lax.dot_general(left, right, (((0,), (0,)), ((), ())), preferred_element_type=f32)


def gather_rows(value, axis):
    count = lax.axis_size(axis)
    blocks = jnp.broadcast_to(value[None], (count,) + value.shape)
    return lax.all_to_all(blocks, axis, 0, 0).reshape((count * value.shape[0],) + value.shape[1:])


def own_block(value, first_row, rows):
    return lax.dynamic_slice(
        value, (first_row, 0), (rows, value.shape[1]), allow_negative_indices=False
    )


def on_chip(kernel, out_shape, scalars, arrays):
    return pl.pallas_call(
        kernel,
        out_shape=out_shape,
        in_specs=[pl.BlockSpec(memory_space=pltpu.SMEM)] * len(scalars)
        + [pl.BlockSpec(memory_space=pltpu.VMEM)] * len(arrays),
        out_specs=[pl.BlockSpec(memory_space=pltpu.VMEM)] * len(out_shape),
        compiler_params=pltpu.CompilerParams(vmem_limit_bytes=40 * 2**20),
    )(*scalars, *arrays)


def chosen_columns(adapter, rows, columns, rank):
    column = lax.broadcasted_iota(jnp.int32, (rows, columns), 1)
    return (column >= adapter * rank) & (column < (adapter + 1) * rank)


def scatter_sum(value, axis):
    count = lax.axis_size(axis)
    blocks = value.astype(jnp.float16).reshape(count, value.shape[0] // count, -1)
    return jnp.sum(lax.all_to_all(blocks, axis, 0, 0).astype(f32), axis=0)


def first_blocks(tokens_far, cotangent_far, sent, tokens, cotangent, done):
    fetch_tokens = pltpu.make_async_copy(tokens_far, tokens, done.at[0])
    fetch_cotangent = pltpu.make_async_copy(cotangent_far, cotangent, done.at[1])
    fetch_tokens.start()
    fetch_cotangent.start()
    fetch_tokens.wait()
    fetch_cotangent.wait()
    width = tokens.shape[1]
    for peer in range(sent.shape[0]):
        sent[peer, :, :width] = tokens[...]
        sent[peer, :, width:] = cotangent[...]


def elementwise(adapter_of_block, scaled, second, rows):
    columns, units = second.shape
    size = scaled.shape[0]
    whole = scaled[...] * (1 / sent_scale)
    adapter = adapter_of_block[lax.rem(lax.axis_index("x"), 2)]
    chosen = chosen_columns(adapter, size, columns, columns // 2)
    low = jnp.where(chosen, whole[:, 3 * units :], 0.0).astype(bf16)
    gate = whole[:, :units]
    grad_hidden = whole[:, 2 * units : 3 * units]
    up = whole[:, units : 2 * units] + adapter_scale * product(low, second[...])
    sig = jax.nn.sigmoid(gate)
    act = gate * sig
    hidden = (act * up).astype(bf16)
    grad_up = (grad_hidden * act).astype(bf16)
    grad_gate = (grad_hidden * up * sig * (1.0 + gate * (1.0 - sig))).astype(bf16)
    for copy in range(rows.shape[0]):
        rows[copy, :, :units] = hidden
        rows[copy, :, units : 2 * units] = grad_gate
        rows[copy, :, 2 * units : 3 * units] = grad_up
        rows[copy, :, 3 * units :] = low


def last_products(adapter_of_block, rows, gate, up, down, second, own, other):
    width, units = gate.shape
    columns = second.shape[0]
    half, quarter = rows.shape[0] // 2, rows.shape[0] // 4
    is_first = lax.axis_index("core") == 0

    def put(value, at):
        low_half, high_half = value[:half], value[half:]
        columns_at = slice(at, at + value.shape[1])
        own[:, columns_at] = jnp.where(is_first, low_half, high_half)
        other[:, columns_at] = jnp.where(is_first, high_half, low_half).astype(bf16)

    grad_up = rows[:, 2 * units : 3 * units]
    value = adapter_scale * trailing_product(grad_up, second[...])
    masks = [
        chosen_columns(adapter_of_block[block % 2], quarter, columns, columns // 2)
        for block in range(4)
    ]
    put(jnp.where(jnp.concatenate(masks, axis=0), value, 0.0), 2 * width)
    grad_gate = rows[:, units : 2 * units]
    for at in range(0, width, 256):
        value = trailing_product(grad_gate, gate[at : at + 256, :])
        put(value + trailing_product(grad_up, up[at : at + 256, :]), width + at)
    for at in range(0, width, 256):
        put(product(rows[:, :units], down[:, at : at + 256]), at)


def core_sum(own, came, sent):
    total = own[...] + came[...].astype(f32)
    peers, rows, _ = sent.shape
    columns = 128
    sums = total.shape[1] - columns
    half = total.shape[0] // 2
    packed = (total[:half, sums:] + total[half:, sums:]).astype(bf16).astype(f32)
    wide = jnp.concatenate(
        [packed[at : at + rows, :] for at in range(0, half, rows)], axis=1
    ).astype(bf16)
    for peer in range(peers):
        sent[peer, :, :sums] = total[peer * rows : (peer + 1) * rows, :sums].astype(bf16)
        sent[peer, :, sums:] = wide


def pipe_sum(came, sums, packed):
    total = came[0].astype(f32)
    for peer in range(1, came.shape[0]):
        total = total + came[peer].astype(f32)
    rows, size = sums.shape
    sums[...] = total[:, :size]
    columns = packed.shape[1]
    packed[...] = jnp.concatenate(
        [total[:, at : at + columns] for at in range(size, total.shape[1], columns)], axis=0
    ).astype(bf16)


def outputs(adapter_of_block, sums, packed, both, first, mixed, grad_tokens, grad_a):
    rows = sums.shape[0]
    columns, width = first.shape
    cores, quarter, _ = packed.shape
    rank = columns // 2
    masks = [
        chosen_columns(adapter_of_block[block], quarter, columns, rank) for block in range(2)
    ]
    core, zlo, y = (lax.axis_index(name) for name in ("core", "zlo", "y"))
    mixed[...] = sums[:, :width].astype(bf16)
    low_own = packed[core, pl.ds(pl.multiple_of(y * rows, rows), rows), :]
    own_mask = chosen_columns(adapter_of_block[zlo], rows, columns, rank)
    low_own = jnp.where(own_mask, low_own.astype(f32), 0.0).astype(bf16)
    grad_tokens[...] = (sums[:, width:] + product(low_own, first[...])).astype(bf16)
    low_back = jnp.concatenate(
        [
            jnp.where(mask, packed[at].astype(f32), 0.0).astype(bf16)
            for at in range(cores)
            for mask in masks
        ],
        axis=0,
    )
    grad_a[...] = leading_product(low_back, both[:, :width])


def on_device(
    tokens,
    gate_weight,
    upward_weight,
    down_weight,
    adapter_first_factors,
    adapter_second_factors,
    adapter_of_block,
    cotangent,
):
    adapters, width, rank = adapter_first_factors.shape
    hidden_units = gate_weight.shape[1]
    columns = adapters * rank
    second = adapter_second_factors.reshape(columns, hidden_units)

    peers, pipe_rows = lax.axis_size(PIPE_LINKS), tokens.shape[0]
    sent = pl.pallas_call(
        first_blocks,
        out_shape=jax.ShapeDtypeStruct((peers, pipe_rows, 2 * width), bf16),
        in_specs=[pl.BlockSpec(memory_space=pl.ANY)] * 2,
        out_specs=pl.BlockSpec(memory_space=pltpu.VMEM),
        scratch_shapes=[pltpu.VMEM(tokens.shape, bf16)] * 2 + [pltpu.SemaphoreType.DMA((2,))],
    )(*(pltpu.with_memory_space_constraint(array, pltpu.HBM) for array in (tokens, cotangent)))
    both = lax.all_to_all(sent, PIPE_LINKS, 0, 0).reshape(peers * pipe_rows, 2 * width)
    both = lax.all_gather(both, "core", axis=0, tiled=True)
    token_rows, adjoint_rows = both[:, :width], both[:, width:]
    row_total = both.shape[0]
    all_columns = 3 * hidden_units + columns

    first_flat = jnp.transpose(adapter_first_factors, (0, 2, 1)).reshape(columns, width)
    parts = jnp.concatenate(
        [
            (product(token_rows, gate_weight) * sent_scale).astype(jnp.float16),
            (product(token_rows, upward_weight) * sent_scale).astype(jnp.float16),
            (trailing_product(adjoint_rows, down_weight) * sent_scale).astype(jnp.float16),
            (trailing_product(token_rows, first_flat) * sent_scale).astype(jnp.float16),
        ],
        axis=1,
    )
    parts = scatter_sum(scatter_sum(parts, "x"), "zhi")
    (rows,) = on_chip(
        elementwise,
        [jax.ShapeDtypeStruct((4, row_total // 16, all_columns), bf16)],
        [adapter_of_block],
        [parts, second],
    )
    rows = lax.all_to_all(rows, "zhi", 0, 0).reshape(row_total // 4, -1)
    rows = gather_rows(rows, "x")

    own, other = on_chip(
        last_products,
        [
            jax.ShapeDtypeStruct((row_total // 2, 2 * width + columns), kind)
            for kind in (f32, bf16)
        ],
        [adapter_of_block],
        [rows, gate_weight, upward_weight, down_weight, second],
    )
    came = lax.ppermute(other, "core", [(0, 1), (1, 0)])
    grad_up_all = rows[:, 2 * hidden_units : 3 * hidden_units]
    grad_b = adapter_scale * leading_product(rows[:, 3 * hidden_units :], grad_up_all)
    grad_b = grad_b.reshape(adapters, rank, hidden_units)
    came, grad_b = lax.optimization_barrier((came, grad_b))

    peers = lax.axis_size(PIPE_LINKS)
    (sent,) = on_chip(
        core_sum,
        [jax.ShapeDtypeStruct((peers, row_total // 2 // peers, 4 * width), bf16)],
        [],
        [own, came],
    )
    came = lax.all_to_all(sent, PIPE_LINKS, 0, 0)
    sums, packed = on_chip(
        pipe_sum,
        [
            jax.ShapeDtypeStruct((tokens.shape[0], 2 * width), f32),
            jax.ShapeDtypeStruct((row_total // 4, columns), bf16),
        ],
        [],
        [came],
    )
    packed = lax.all_gather(packed, "core", axis=0)
    mixed, grad_tokens, grad_a = on_chip(
        outputs,
        [
            jax.ShapeDtypeStruct((tokens.shape[0], width), bf16),
            jax.ShapeDtypeStruct((tokens.shape[0], width), bf16),
            jax.ShapeDtypeStruct((columns, width), f32),
        ],
        [adapter_of_block],
        [sums, packed, both, first_flat],
    )
    grad_a = jnp.transpose(grad_a.reshape(adapters, rank, width), (0, 2, 1))
    return mixed, grad_tokens, grad_a, grad_b


def solution(mesh):
    parts = Mesh(mesh.devices.reshape(2, 8, 2, 4, 4), PIPE + TENSOR)
    in_specs = (
        P(PIPE, TENSOR),
        P(TENSOR, PIPE),
        P(TENSOR, PIPE),
        P(PIPE, TENSOR),
        P(None, TENSOR, None),
        P(None, None, PIPE),
        P(),
        P(PIPE, TENSOR),
    )
    out_specs = (
        P(PIPE, TENSOR),
        P(PIPE, TENSOR),
        P(None, TENSOR, None),
        P(None, None, PIPE),
    )
    return jax.shard_map(
        on_device, mesh=parts, in_specs=in_specs, out_specs=out_specs, check_vma=False
    )
```
